256 devices in a mesh: slab: 64 (over z, x, core), dom: 4 (over y).
Axes of the slice: x: 4, y: 4, z: 8, core: 2. Of those that a mesh axis runs over, the one named last changes fastest.
Arguments:
- elem_grad: float32 [3, 8, 1376256], P(None, None, ('slab', 'dom')), may hold values from -3 to 3
- elem_stress: float32 [6, 1376256], P(None, ('slab', 'dom')), may hold values from -6 to 6
- elem_grade: int32 [1376256], P(('slab', 'dom')), may hold values from 0 to 15
- grade_scale: float32 [16], replicated, may hold values from 0.5 to 2
- part_counts: int32 [64, 4], P('slab'), may hold values from 1 to 5376, as said below
- node_lists: int32 [4, 128, 8, 512], P(None, 'slab', None, 'dom'), may hold values from -1 to 7167, as said below
- stiff_diag: float32 [3, 128, 8, 512], P(None, 'slab', None, 'dom'), may hold values from 1 to 4
- start_block: float32 [3, 32, 128, 8, 512], P(None, None, 'slab', None, 'dom'), may hold values from -600 to 600
Outputs:
- next_block: float32 [3, 32, 128, 8, 512], P(None, None, 'slab', None, 'dom')
- diag_blocks: float32 [2, 32, 32], replicated
- offdiag_blocks: float32 [3, 32, 32], replicated
The draws below stay inside these ranges and needn't reach their ends.
Inputs may be any that keep to these rules, and one draw needn't show every extreme that they name: `part_counts`: each row sums to 7168, the elements of one slab; in every slab one partition holds exactly 5376. node_lists[j, f, x, y] is the pool number, within the slab of floor f, of the element of layer f whose in-plane base corner is (x - j mod 2, (y - j // 2) mod 512); it is -1 exactly where x - j mod 2 lies outside 0 to 6. Every element of a slab appears at its four in-plane corners.
All inputs are finite; a program needn't handle non-finite values.
Results may differ from the reference program's by a relative error of at most 0.0003.
Values sent between devices are 32-bit elements; how exact they have to be, the bound alone decides.
No kernel may reach another device: no remote copies, remote signals or barrier semaphores. Data moves between devices by JAX's collectives and lax.ppermute only.
A program may use at most 128 MiB of HBM per device.

```python
import math
import jax
import jax.numpy as jnp
import numpy as np
from jax import lax

VECS = 32
MATS = 16
GX = 8
GYD = 128
FLOORS_DEV = 2
GY = 512
FLOORS = 128
E_CAP = 5376
ELEMS = 1376256
N_SLAB = 64
N_DOM = 4


def slab_layout(key):
    layout_key = jax.random.fold_in(key, 17)
    heavy_key, weight_key, order_key = jax.random.split(layout_key, 3)
    per_part = FLOORS_DEV * (GX - 1) * GYD
    slab_total = per_part * N_DOM
    spare_total = slab_total - E_CAP
    heavy_part = jax.random.randint(heavy_key, (N_SLAB, 1), 0, N_DOM)
    weights = jax.random.randint(weight_key, (N_SLAB, N_DOM - 1), 1, 5)
    shares = spare_total * weights // jnp.sum(weights, axis=1, keepdims=True)
    shares = shares.at[:, -1].add(spare_total - jnp.sum(shares, axis=1))
    places = jnp.arange(N_DOM)[None, :]
    other_rank = jnp.clip(places - (places > heavy_part).astype(jnp.int32), 0, N_DOM - 2)
    counts = jnp.where(places == heavy_part, E_CAP, jnp.take_along_axis(shares, other_rank, axis=1))
    slab_keys = jax.random.split(order_key, N_SLAB)
    orders = jax.vmap(lambda slab_key: jax.random.permutation(slab_key, slab_total))(slab_keys)
    return (counts.astype(jnp.int32), orders.astype(jnp.int32))


def draw_part_counts(key, part):
    return slab_layout(key)[0]


def draw_node_lists(key, part):
    orders = slab_layout(key)[1]
    quad_slot = jnp.arange(4).reshape(4, 1, 1, 1)
    floor_index = jnp.arange(FLOORS).reshape(1, FLOORS, 1, 1)
    across = jnp.arange(GX).reshape(1, 1, GX, 1)
    beside_all = jnp.arange(GY).reshape(1, 1, 1, GY)
    base_x = across - quad_slot % 2
    base_y = (beside_all - quad_slot // 2) % GY
    inside = (base_x >= 0) & (base_x <= GX - 2)
    layer_index = floor_index % FLOORS_DEV
    slab_index = floor_index // FLOORS_DEV
    structured = layer_index * ((GX - 1) * GY) + jnp.clip(base_x, 0, GX - 2) * GY + base_y
    pool_ids = orders[slab_index, structured]
    return jnp.where(inside, pool_ids, -1).astype(jnp.int32)


def draw_start_block(key, part):
    node_key, vector_key, noise_key = jax.random.split(jax.random.fold_in(key, 29), 3)
    block_shape = (3, VECS, FLOORS, GX, GY)
    node_scale = jnp.exp(jax.random.uniform(node_key, (1, 1, FLOORS, GX, GY), jnp.float32) * math.log(10.0))
    vector_scale = jnp.exp(jax.random.uniform(vector_key, (1, VECS, 1, 1, 1), jnp.float32) * math.log(10.0))
    values = jnp.clip(jax.random.normal(noise_key, block_shape, jnp.float32), -6.0, 6.0)
    return (values * node_scale * vector_scale).astype(jnp.float32)


def with_ends(values, rng, low, top_value):
    place = [jax.random.randint(jax.random.fold_in(rng, axis), (), 0, length) for axis, length in enumerate(values.shape)]
    main_axis = values.shape.index(max(values.shape))
    neighbour = place[:main_axis] + [(place[main_axis] + 1) % values.shape[main_axis]] + place[main_axis + 1:]
    return values.at[tuple(place)].set(low).at[tuple(neighbour)].set(top_value)


def block_scale(own_key, extent, shards, low, high):
    level = 1.0
    for position, blocks in shards:
        draws = jax.random.uniform(jax.random.fold_in(jax.random.fold_in(own_key, 6), position), (blocks,), jnp.float32, low / len(shards), high / len(shards))
        level = level * jnp.repeat(jnp.exp(draws), extent[position] // blocks).reshape((-1,) + (1,) * (len(extent) - 1 - position))
    return level


def bell_draw(stream_key, dims, deviation, reach, shards=(), kind=jnp.bfloat16):
    level = block_scale(stream_key, dims, shards, -0.22, 0.18) if shards else 1.0
    drawn = jax.random.normal(stream_key, dims, jnp.float32) * deviation * level
    return jnp.minimum(jnp.maximum(drawn, -reach), reach).astype(kind)


def setup_inputs(seed: int = 0) -> dict:
    arg_keys = jax.random.split(jax.random.key(seed), 9)
    elem_grad = bell_draw(arg_keys[0], (3, 8, ELEMS), 0.5, 3.0, ((2, 256),), jnp.float32)
    elem_stress = bell_draw(arg_keys[1], (6, ELEMS), 1.0, 6.0, ((1, 256),), jnp.float32)
    elem_grade = with_ends(jax.random.randint(arg_keys[2], (ELEMS,), 0, MATS), jax.random.fold_in(arg_keys[2], 1), 0, MATS - 1).astype(jnp.int32)
    grade_scale = jnp.clip(jnp.exp(jax.random.uniform(arg_keys[3], (MATS,), jnp.float32, math.log(0.5), math.log(2.0))), 0.5, 2.0)
    part_counts = draw_part_counts(jax.random.fold_in(arg_keys[8], 71), 0)
    node_lists = draw_node_lists(jax.random.fold_in(arg_keys[8], 71), 0)
    stiff_diag = jnp.clip(jnp.exp(math.log(4.0) - 1.3862944 * jax.random.uniform(arg_keys[6], (3, FLOORS, GX, GY), jnp.float32) ** block_scale(arg_keys[6], (3, FLOORS, GX, GY), ((1, 64), (3, 4)), -0.2, 0.2)), 1.0, 4.0)
    start_block = draw_start_block(jax.random.fold_in(arg_keys[8], 71), 0)
    return {"elem_grad": elem_grad, "elem_stress": elem_stress, "elem_grade": elem_grade, "grade_scale": grade_scale, "part_counts": part_counts, "node_lists": node_lists, "stiff_diag": stiff_diag, "start_block": start_block}


highest = lax.Precision.HIGHEST

def offset_table(quad_slot, layer_side):
    table = np.zeros((8, 27))
    shift_x = quad_slot % 2
    shift_y = quad_slot // 2
    for corner in range(8):
        corner_x = corner % 2
        corner_y = corner // 2 % 2
        corner_z = corner // 4
        target = corner_x - shift_x + 1 + 3 * (corner_y - shift_y + 1) + 9 * (corner_z - layer_side + 1)
        table[corner, target] = 1.0
    return jnp.asarray(table, dtype=jnp.float32)

def stress_matrix(stress):
    return jnp.stack([jnp.stack([stress[0], stress[5], stress[4]]), jnp.stack([stress[5], stress[1], stress[3]]), jnp.stack([stress[4], stress[3], stress[2]])])

def grade_lookup(grades, table):
    levels = jnp.arange(table.shape[0], dtype=jnp.int32)[:, None]
    onehot = (grades[None, :] == levels).astype(jnp.float32)
    return jnp.dot(table, onehot, precision=highest)

def element_matrices(gradients, stress, scales):
    pushed = jnp.einsum('ik...,kb...->ib...', stress_matrix(stress), gradients, precision=highest)
    return jnp.einsum('ia...,ib...->ab...', gradients, pushed, precision=highest) * scales

def pool_columns(slot_lists, counts, capacity):
    offsets = (jnp.cumsum(counts) - counts).astype(jnp.int32)
    shaped = offsets.reshape((-1,) + (1,) * slot_lists.ndim)
    pool_ids = jnp.maximum(slot_lists, 0)
    partition = jnp.sum((pool_ids[None] >= shaped[1:]).astype(jnp.int32), axis=0).astype(jnp.int32)
    levels = jnp.arange(counts.shape[0], dtype=jnp.int32).reshape(shaped.shape)
    starts = jnp.sum(jnp.where(partition[None] == levels, shaped, 0), axis=0).astype(jnp.int32)
    columns = partition * capacity + pool_ids - starts
    return (columns.astype(jnp.int32), (slot_lists >= 0).astype(jnp.float32))

def accumulate(getter, present):
    sides = []
    for layer_side in range(2):
        summed = None
        for quad_slot in range(4):
            row_values = getter(quad_slot, layer_side) * present[quad_slot]
            contribution = jnp.einsum('bfxy,bo->ofxy', row_values, offset_table(quad_slot, layer_side), precision=highest)
            summed = contribution if summed is None else summed + contribution
        sides.append(summed)
    return (sides[0], sides[1])

def slab_sides(gradients, stress, grades, scale_table, counts, slot_lists):
    capacity = gradients.shape[-1] // counts.shape[0]
    matrices = element_matrices(gradients, stress, grade_lookup(grades, scale_table))
    columns, present = pool_columns(slot_lists, counts, capacity)
    picked = jnp.take(matrices.reshape(64, -1), columns.reshape(-1), axis=1)
    picked = picked.reshape((8, 8) + slot_lists.shape)

    def getter(quad_slot, layer_side):
        return picked[quad_slot + 4 * layer_side, :, quad_slot]
    return accumulate(getter, present)

def apply_operator(block, stencil, diagonal):
    wrapped = jnp.concatenate([block[..., -1:], block, block[..., :1]], axis=-1)
    padded = jnp.pad(wrapped, ((0, 0), (0, 0), (1, 1), (1, 1), (0, 0)))
    floors, across, beside_all = (block.shape[2], block.shape[3], block.shape[4])
    result = diagonal[:, None] * block
    for offset in range(27):
        step_x = offset % 3
        step_y = offset // 3 % 3
        step_z = offset // 9
        result = result + stencil[offset] * padded[:, :, step_z:step_z + floors, step_x:step_x + across, step_y:step_y + beside_all]
    return result

def inner(first_block, second_block):
    dof_count = 3 * FLOORS * GX * GY
    return jnp.einsum('cvfxy,cwfxy->vw', first_block, second_block, precision=highest) / dof_count

def mix(block, matrix):
    return jnp.einsum('cvfxy,vw->cwfxy', block, matrix, precision=highest)

def normalize(block, gram_matrix):
    factor = jnp.linalg.cholesky(gram_matrix)
    identity = jnp.eye(gram_matrix.shape[0], dtype=jnp.float32)
    inverse = lax.linalg.triangular_solve(factor, identity, left_side=True, lower=True)
    return (jnp.einsum('cvfxy,wv->cwfxy', block, inverse, precision=highest), factor.T)

def reference(elem_grad, elem_stress, elem_grade, grade_scale, part_counts, node_lists, stiff_diag, start_block):
    pool_width = N_DOM * E_CAP
    gradients = jnp.moveaxis(elem_grad.reshape(3, 8, N_SLAB, pool_width), 2, 0)
    stresses = jnp.moveaxis(elem_stress.reshape(6, N_SLAB, pool_width), 1, 0)
    grades = elem_grade.reshape(N_SLAB, pool_width)
    slot_lists = jnp.moveaxis(node_lists.reshape(4, N_SLAB, FLOORS_DEV, GX, GY), 1, 0)

    def per_slab(slab_items):
        return slab_sides(slab_items[0], slab_items[1], slab_items[2], grade_scale, slab_items[3], slab_items[4])
    bottom, top_side = lax.map(per_slab, (gradients, stresses, grades, part_counts, slot_lists))
    bottom = jnp.moveaxis(bottom, 0, 1).reshape(27, FLOORS, GX, GY)
    top_side = jnp.moveaxis(top_side, 0, 1).reshape(27, FLOORS, GX, GY)
    stencil = top_side + jnp.concatenate([bottom[:, 1:], jnp.zeros((27, 1, GX, GY), jnp.float32)], axis=1)
    first, start_factor = normalize(start_block, inner(start_block, start_block))
    image_block = apply_operator(first, stencil, stiff_diag)
    alpha_one = inner(first, image_block)
    residual = image_block - mix(first, alpha_one)
    second, beta_one = normalize(residual, inner(residual, residual))
    image_block = apply_operator(second, stencil, stiff_diag) - mix(first, beta_one.T)
    alpha_two = inner(second, image_block)
    residual = image_block - mix(second, alpha_two)
    third, beta_two = normalize(residual, inner(residual, residual))
    return (third, jnp.stack([alpha_one, alpha_two]), jnp.stack([start_factor, beta_one, beta_two]))
```

```python
import jax
import jax.numpy as jnp
from jax import lax
from jax.experimental import pallas as pl
from jax.experimental.pallas import tpu as pltpu
from jax.sharding import PartitionSpec as P

highest = lax.Precision.HIGHEST
SUB, LANE = 8, 128
ROWS = 31


def lane_pick(values, index):
    return jnp.take_along_axis(values, index, axis=1, mode="promise_in_bounds")


def stencil_kernel(ranges_ref, table_ref, lists_ref, *refs):
    sources, (low_ref, top_ref, below_ref, picked_ref) = refs[:-4], refs[-4:]
    sub = lax.broadcasted_iota(jnp.int32, (SUB, LANE), 0)
    lane = lax.broadcasted_iota(jnp.int32, (SUB, LANE), 1)
    inner = sub < SUB - 1
    ids = []
    for layer in range(2):
        behind = jnp.broadcast_to(lists_ref[2, layer, :, 0:1], (SUB, LANE))
        behind = jnp.max(jnp.where(lane == sub, behind, -1), axis=0, keepdims=True)
        behind = jnp.broadcast_to(behind, (SUB, LANE))
        behind = jnp.where(lane < SUB - 1, behind, -1)
        ids.append(jnp.where(inner, lists_ref[0, layer], behind))
    picked_ref[...] = jnp.zeros(picked_ref.shape, jnp.float32)
    for part in range(len(sources) // 2):
        start, count = ranges_ref[part, 0], ranges_ref[part, 1]
        group_of, lane_of = [], []
        for layer in range(2):
            place = ids[layer] - start
            held = (place >= 0) & (place < count)
            group_of.append(jnp.where(held, place >> 7, -1))
            lane_of.append(jnp.where(held, place & (LANE - 1), 0))
        halves = sources[2 * part : 2 * part + 2]

        def pick_groups(step, carry):
            for unit in range(2):
                group = step * 2 + unit
                span = pl.ds(pl.multiple_of(group * LANE, LANE), LANE)
                here = [group_of[layer] == group for layer in range(2)]
                for row in range(ROWS):
                    half, line = divmod(row, 16)
                    line = jnp.broadcast_to(halves[half][line : line + 1, span], (SUB, LANE))
                    for layer in range(2):
                        got = lane_pick(line, lane_of[layer])
                        picked_ref[layer, row] = jnp.where(here[layer], got, picked_ref[layer, row])
            return carry

        lax.fori_loop(0, (count + 2 * LANE - 1) // (2 * LANE), pick_groups, 0)
    low_ref[...] = jnp.zeros(low_ref.shape, jnp.float32)
    top_ref[...] = jnp.zeros(top_ref.shape, jnp.float32)
    below_ref[...] = jnp.zeros(below_ref.shape, jnp.float32)
    first_lane = lane == 0

    def from_behind(rows):
        edge = lane_pick(jnp.broadcast_to(rows[SUB - 1 : SUB], (SUB, LANE)), sub)
        return jnp.where(first_lane, edge, pltpu.roll(rows, 1, axis=1))

    for layer in range(2):
        grade = picked_ref[layer, 30]
        scale = jnp.zeros((SUB, LANE), jnp.float32)
        for level in range(table_ref.shape[0]):
            scale = jnp.where(grade == float(level), table_ref[level], scale)
        own = [picked_ref[layer, row] for row in range(24)]
        own += [picked_ref[layer, 24 + row] * scale for row in range(6)]
        behind = [from_behind(rows) for rows in own]
        for slot in range(4):
            data = own if slot < 2 else behind
            stress = [jnp.where(inner, data[24 + row], 0.0) for row in range(6)]
            grad = data[:24]
            if slot % 2 == 1:
                stress = [pltpu.roll(rows, 1, axis=0) for rows in stress]
                grad = [pltpu.roll(rows, 1, axis=0) for rows in grad]
            order = ((0, 5, 4), (5, 1, 3), (4, 3, 2))
            for corner in range(8):
                pushed = [
                    stress[order[i][0]] * grad[corner]
                    + stress[order[i][1]] * grad[8 + corner]
                    + stress[order[i][2]] * grad[16 + corner]
                    for i in range(3)
                ]
                offset = (corner % 2 - slot % 2 + 1) + 3 * (corner // 2 % 2 - slot // 2 + 1)
                offset += 9 * (corner // 4)
                upper = sum(grad[8 * i + slot + 4] * pushed[i] for i in range(3))
                lower = sum(grad[8 * i + slot] * pushed[i] for i in range(3))
                if layer == 0:
                    low_ref[offset] += upper
                    below_ref[offset] += lower
                else:
                    top_ref[offset] += upper
                    low_ref[offset + 9] += lower
    for ref in (low_ref, top_ref, below_ref):
        for offset in range(ref.shape[0]):
            if offset % 3 != 1:
                ref[offset] = pltpu.roll(ref[offset], (offset % 3 - 1) % SUB, axis=0)


def local_stencils(ranges, table, lists, sources):
    vmem = pl.BlockSpec(memory_space=pltpu.VMEM)
    smem = pl.BlockSpec(memory_space=pltpu.SMEM)
    return pl.pallas_call(
        stencil_kernel,
        out_shape=[
            jax.ShapeDtypeStruct((27, SUB, LANE), jnp.float32),
            jax.ShapeDtypeStruct((18, SUB, LANE), jnp.float32),
            jax.ShapeDtypeStruct((18, SUB, LANE), jnp.float32),
        ],
        in_specs=[smem, smem] + [vmem] * (1 + len(sources)),
        out_specs=[vmem, vmem, vmem],
        scratch_shapes=[pltpu.VMEM((2, ROWS, SUB, LANE), jnp.float32)],
        compiler_params=pltpu.CompilerParams(vmem_limit_bytes=24 * 1024 * 1024),
    )(ranges, table, lists, *sources)


def edges_kernel(first_ref, second_ref, left_ref, right_ref):
    collect_edges((first_ref, second_ref), left_ref, right_ref)


def collect_edges(floors, left_ref, right_ref):
    lane = lax.broadcasted_iota(jnp.int32, (SUB, LANE), 1)
    vecs = floors[0].shape[0]

    def step(vec, carry):
        out = []
        for floor in range(2):
            rows = floors[floor][vec]
            left, right = carry[2 * floor : 2 * floor + 2]
            out.append(jnp.where(lane == vec, pltpu.roll(rows, vec, axis=1), left))
            out.append(jnp.where(lane == vec, pltpu.roll(rows, vec + 1, axis=1), right))
        return tuple(out)

    zero = jnp.zeros((SUB, LANE), jnp.float32)
    done = lax.fori_loop(0, vecs, step, (zero,) * 4, unroll=4)
    for floor in range(2):
        left_ref[floor] = done[2 * floor]
        right_ref[floor] = done[2 * floor + 1]


def edge_columns(first, second):
    vmem = pl.BlockSpec(memory_space=pltpu.VMEM)
    shape = jax.ShapeDtypeStruct((2, SUB, LANE), jnp.float32)
    return pl.pallas_call(
        edges_kernel, out_shape=[shape, shape], in_specs=[vmem] * 2, out_specs=[vmem] * 2
    )(first, second)


def operator_rows(floors, behind, ahead, low_ref, high_ref, diag_ref, outs, edges):
    lane = lax.broadcasted_iota(jnp.int32, (SUB, LANE), 1)
    vecs = floors[0].shape[0]
    per_comp = vecs // diag_ref.shape[0]
    width = 2

    def step(index, carry):
        base = index * width
        rows = []
        for unit in range(width):
            vec = base + unit
            for z in range(4):
                mid = floors[z][vec]
                left = pltpu.roll(behind[z], LANE - vec, axis=1)
                left = jnp.where(lane == 0, left, pltpu.roll(mid, 1, axis=1))
                right = pltpu.roll(ahead[z], LANE - 1 - vec, axis=1)
                right = jnp.where(lane == LANE - 1, right, pltpu.roll(mid, LANE - 1, axis=1))
                rows.append((left, mid, right))
        new = list(carry)
        comp = base // per_comp
        for floor, stencil_ref in ((0, low_ref), (1, high_ref)):
            weight = diag_ref[comp, floor]
            sums = [[None] * 3 for _ in range(width)]
            for offset in range(27):
                taps = stencil_ref[offset]
                dx, dy, dz = offset % 3, offset // 3 % 3, offset // 9
                for unit in range(width):
                    term = taps * rows[4 * unit + floor + dz][dy]
                    old = sums[unit][dx]
                    sums[unit][dx] = term if old is None else old + term
            for unit in range(width):
                vec = base + unit
                total = weight * rows[4 * unit + floor + 1][1] + sums[unit][1]
                total = total + pltpu.roll(sums[unit][0], 1, axis=0)
                total = total + pltpu.roll(sums[unit][2], SUB - 1, axis=0)
                outs[floor][vec] = total
                if edges is not None:
                    new[2 * floor] = jnp.where(
                        lane == vec, pltpu.roll(total, vec, axis=1), new[2 * floor]
                    )
                    new[2 * floor + 1] = jnp.where(
                        lane == vec, pltpu.roll(total, vec + 1, axis=1), new[2 * floor + 1]
                    )
        return tuple(new)

    zero = jnp.zeros((SUB, LANE), jnp.float32)
    done = lax.fori_loop(0, vecs // width, step, (zero,) * (0 if edges is None else 4))
    if edges is not None:
        for floor in range(2):
            edges[0][floor] = done[2 * floor]
            edges[1][floor] = done[2 * floor + 1]


def first_operator_kernel(
    under_ref, first_ref, second_ref, over_ref, behind_ref, ahead_ref, low_ref, top_ref, below_ref,
    diag_ref, out_0_ref, out_1_ref, left_ref, right_ref, high_ref,
):
    high_ref[0:18] = top_ref[...]
    high_ref[18:27] = below_ref[9:18]
    high_ref[9:18] = high_ref[9:18] + below_ref[0:9]
    operator_rows(
        (under_ref, first_ref, second_ref, over_ref),
        [behind_ref[z] for z in range(4)],
        [ahead_ref[z] for z in range(4)],
        low_ref, high_ref, diag_ref, (out_0_ref, out_1_ref), (left_ref, right_ref),
    )


def second_operator_kernel(
    under_ref, first_ref, second_ref, over_ref, behind_ref, ahead_ref, low_ref, high_ref, diag_ref,
    start_0_ref, start_1_ref, out_0_ref, out_1_ref, gram_ref,
):
    operator_rows(
        (under_ref, first_ref, second_ref, over_ref),
        [behind_ref[z] for z in range(4)],
        [ahead_ref[z] for z in range(4)],
        low_ref, high_ref, diag_ref, (out_0_ref, out_1_ref), None,
    )
    blocks = ((start_0_ref, first_ref, out_0_ref), (start_1_ref, second_ref, out_1_ref))
    vecs = first_ref.shape[0] // diag_ref.shape[0]
    gram = None
    for comp in range(diag_ref.shape[0]):
        for floor in range(2):
            for across in range(0, SUB, 2):
                rows = []
                for ref in blocks[floor]:
                    span = pl.ds(comp * vecs, vecs)
                    rows.append(
                        jnp.concatenate([ref[span, across, :], ref[span, across + 1, :]], axis=1)
                    )
                rows = jnp.concatenate(rows, axis=0)
                term = lax.dot_general(
                    rows, rows, (((1,), (1,)), ((), ())), precision=highest,
                    preferred_element_type=jnp.float32,
                )
                gram = term if gram is None else gram + term
    gram_ref[...] = gram


def call_whole(kernel, out_shape, *operands, scratch_shapes=()):
    vmem = pl.BlockSpec(memory_space=pltpu.VMEM)
    return pl.pallas_call(
        kernel,
        out_shape=out_shape,
        in_specs=[vmem] * len(operands),
        out_specs=[vmem] * len(out_shape),
        scratch_shapes=scratch_shapes,
        compiler_params=pltpu.CompilerParams(vmem_limit_bytes=32 * 1024 * 1024),
    )(*operands)


def apply_first(under, first, second, over, behind, ahead, low, top, below, diagonal):
    floor = jax.ShapeDtypeStruct(first.shape, jnp.float32)
    edge = jax.ShapeDtypeStruct((2, SUB, LANE), jnp.float32)
    taps = jax.ShapeDtypeStruct((27, SUB, LANE), jnp.float32)
    return call_whole(
        first_operator_kernel, [floor, floor, edge, edge, taps],
        under, first, second, over, behind, ahead, low, top, below, diagonal,
    )


def apply_second(under, first, second, over, behind, ahead, low, high, diagonal, start_0, start_1):
    floor = jax.ShapeDtypeStruct(first.shape, jnp.float32)
    size = 3 * first.shape[0] // diagonal.shape[0]
    gram = jax.ShapeDtypeStruct((size, size), jnp.float32)
    return call_whole(
        second_operator_kernel, [floor, floor, gram],
        under, first, second, over, behind, ahead, low, high, diagonal, start_0, start_1,
    )


def dot_rows(left, right):
    return lax.dot_general(
        left, right, (((1,), (0,)), ((), ())), precision=highest, preferred_element_type=jnp.float32
    )


def dot_both(left, right):
    return lax.dot_general(
        left, right, (((1,), (1,)), ((), ())), precision=highest, preferred_element_type=jnp.float32
    )


def eliminate(gram):
    size = gram.shape[0]
    row_id = lax.broadcasted_iota(jnp.int32, (size, 2 * size), 0)
    lane_id = lax.broadcasted_iota(jnp.int32, (size, 2 * size), 1)
    identity = (row_id[:, :size] == lane_id[:, :size]).astype(jnp.float32)
    work = jnp.concatenate([gram, identity], axis=1)
    for k in range(size):
        inverse = 1.0 / jnp.sqrt(work[k : k + 1, k : k + 1])
        row = work[k : k + 1, :] * inverse
        column = work[:, k : k + 1] * inverse
        work = jnp.where(row_id == k, row, jnp.where(row_id > k, work - column * row, work))
    upper = jnp.where(row_id[:, :size] <= lane_id[:, :size], work[:, :size], 0.0)
    return upper, work[:, size:]


def finish_kernel(gram_ref, *refs):
    blocks = (refs[0:5:2], refs[1:6:2])
    next_ref, diag_ref, offdiag_ref = refs[6:]
    vecs = diag_ref.shape[1]
    comps = next_ref.shape[0]
    zero = jnp.zeros((vecs, vecs), jnp.float32)
    eye = (
        lax.broadcasted_iota(jnp.int32, (vecs, vecs), 0)
        == lax.broadcasted_iota(jnp.int32, (vecs, vecs), 1)
    ).astype(jnp.float32)

    def grid(rows):
        return jnp.concatenate([jnp.concatenate(row, axis=1) for row in rows], axis=0)

    def block(matrix, row, column):
        return matrix[row * vecs : (row + 1) * vecs, column * vecs : (column + 1) * vecs]

    gram = gram_ref[...]
    upper_0, inverse_0 = eliminate(block(gram, 0, 0))
    spread = grid([[inverse_0, zero, zero], [zero, inverse_0, zero], [zero, zero, inverse_0]])
    krylov = dot_both(dot_rows(spread, gram), spread)
    alpha_1, alpha_1_t = block(krylov, 0, 1), block(krylov, 1, 0)
    change = grid([[eye, zero, zero], [-alpha_1_t, eye, zero], [zero, -alpha_1_t, eye]])
    moved = dot_both(dot_rows(change, krylov), change)
    upper_1, inverse_1 = eliminate(block(moved, 1, 1))
    second = grid([[zero, inverse_1, zero], [-upper_1, zero, inverse_1]])
    products = dot_both(dot_rows(second, moved), second)
    alpha_2, alpha_2_t = block(products, 0, 1), block(products, 1, 0)
    upper_2, inverse_2 = eliminate(block(products, 1, 1) - dot_rows(alpha_2_t, alpha_2))
    residual = jnp.concatenate([-upper_1, -dot_rows(alpha_2_t, inverse_1), inverse_1], axis=1)
    coefs = dot_rows(dot_rows(dot_rows(inverse_2, residual), change), spread)
    diag_ref[0] = alpha_1
    diag_ref[1] = alpha_2
    offdiag_ref[0] = upper_0
    offdiag_ref[1] = upper_1
    offdiag_ref[2] = upper_2
    for comp in range(comps):
        for floor in range(2):
            span = pl.ds(comp * vecs, vecs)
            for across in range(0, SUB, 2):
                rows = jnp.concatenate(
                    [
                        jnp.concatenate([ref[span, across, :], ref[span, across + 1, :]], axis=1)
                        for ref in blocks[floor]
                    ],
                    axis=0,
                )
                mixed = dot_rows(coefs, rows)
                next_ref[comp, :, floor, across, :] = mixed[:, :LANE]
                next_ref[comp, :, floor, across + 1, :] = mixed[:, LANE:]


def finish(gram, blocks, out_shape, vecs):
    return call_whole(
        finish_kernel,
        [
            jax.ShapeDtypeStruct(out_shape, jnp.float32),
            jax.ShapeDtypeStruct((2, vecs, vecs), jnp.float32),
            jax.ShapeDtypeStruct((3, vecs, vecs), jnp.float32),
        ],
        gram, *blocks,
    )


def exchange(value, axis, route):
    size = lax.axis_size(axis)
    return lax.ppermute(value, axis, [(i, route(i)) for i in range(size)])


def ring_pairs(stride, size, odd_first):
    def route(i):
        digit = i // stride % size
        if odd_first:
            partner = (digit + 1) % size if digit % 2 == 0 else (digit - 1) % size
        else:
            partner = (digit + 1) % size if digit % 2 == 1 else (digit - 1) % size
        return i + (partner - digit) * stride

    return route


def far_pairs(stride):
    partners = (3, 6, 5, 0, 7, 2, 1, 4)

    def route(i):
        digit = i // stride % 8
        return i + (partners[digit] - digit) * stride

    return route


def mesh_sum(value):
    steps = [
        ("slab", ring_pairs(1, 2, True)),
        ("dom", ring_pairs(1, 4, True)),
        ("dom", ring_pairs(1, 4, False)),
        ("slab", ring_pairs(2, 4, True)),
        ("slab", ring_pairs(2, 4, False)),
        ("slab", ring_pairs(8, 8, True)),
        ("slab", ring_pairs(8, 8, False)),
        ("slab", far_pairs(8)),
    ]
    for axis, route in steps:
        value = value + exchange(value, axis, route)
    return value


def shifted(value, axis, steps, wrap):
    size = lax.axis_size(axis)
    route = [(i, (i + steps) % size) for i in range(size) if wrap or 0 <= i + steps < size]
    return lax.ppermute(value, axis, route)


def beside(first, second, left, right):
    from_left = shifted(right, "dom", 1, True)
    from_right = shifted(left, "dom", -1, True)
    under = shifted(second, "slab", 1, False)
    over = shifted(first, "slab", -1, False)
    up = shifted(jnp.stack([from_left[1], from_right[1]]), "slab", 1, False)
    down = shifted(jnp.stack([from_left[0], from_right[0]]), "slab", -1, False)
    behind = jnp.concatenate([up[0:1], from_left, down[0:1]], axis=0)
    ahead = jnp.concatenate([up[1:2], from_right, down[1:2]], axis=0)
    return under, over, behind, ahead


def gathered(elem_grad, elem_stress, elem_grade):
    capacity = elem_grad.shape[2]
    packed = jnp.concatenate(
        [
            elem_grad.reshape(24, capacity),
            elem_stress,
            elem_grade.astype(jnp.float32)[None],
            jnp.zeros((1, capacity), jnp.float32),
        ],
        axis=0,
    )
    low, high = packed[:16], packed[16:]
    low_1, high_1 = shifted(low, "dom", 1, True), shifted(high, "dom", 1, True)
    low_3, high_3 = shifted(low, "dom", -1, True), shifted(high, "dom", -1, True)
    low_2, high_2 = shifted(low_1, "dom", 1, True), shifted(high_3, "dom", -1, True)
    return [low, high, low_1, high_1, low_2, high_2, low_3, high_3]


def per_device(
    elem_grad,
    elem_stress,
    elem_grade,
    grade_scale,
    part_counts,
    node_lists,
    stiff_diag,
    start_block,
):
    comps, vecs = start_block.shape[:2]
    floor_shape = (comps * vecs,) + start_block.shape[3:]
    sources = gathered(elem_grad, elem_stress, elem_grade)
    counts = part_counts[0]
    starts = jnp.cumsum(counts) - counts
    parts = lax.axis_size("dom")
    order = (lax.axis_index("dom") - jnp.arange(parts, dtype=jnp.int32)) % parts
    ranges = jnp.stack([starts[order], counts[order]], axis=1).astype(jnp.int32)
    start_0 = start_block[:, :, 0].reshape(floor_shape)
    start_1 = start_block[:, :, 1].reshape(floor_shape)
    under, over, behind, ahead = beside(start_0, start_1, *edge_columns(start_0, start_1))
    low, top, below = local_stencils(ranges, grade_scale, node_lists, sources)
    below = shifted(below, "slab", -1, False)
    image_0, image_1, left, right, high = apply_first(
        under, start_0, start_1, over, behind, ahead, low, top, below, stiff_diag
    )
    under, over, behind, ahead = beside(image_0, image_1, left, right)
    second_0, second_1, gram = apply_second(
        under, image_0, image_1, over, behind, ahead, low, high, stiff_diag, start_0, start_1
    )
    dof_count = (
        start_block.size // vecs * lax.axis_size("slab") * lax.axis_size("dom")
    )
    gram = mesh_sum(gram) / dof_count
    blocks = (start_0, start_1, image_0, image_1, second_0, second_1)
    return finish(gram, blocks, start_block.shape, vecs)


def solution(mesh):
    in_specs = (
        P(None, None, ("slab", "dom")),
        P(None, ("slab", "dom")),
        P(("slab", "dom")),
        P(),
        P("slab", None),
        P(None, "slab", None, "dom"),
        P(None, "slab", None, "dom"),
        P(None, None, "slab", None, "dom"),
    )
    out_specs = (P(None, None, "slab", None, "dom"), P(), P())
    return jax.shard_map(
        per_device, mesh=mesh, in_specs=in_specs, out_specs=out_specs, check_vma=False
    )
```

```python
import jax
import jax.numpy as jnp
from jax import lax
from jax.experimental import pallas as pl
from jax.experimental.pallas import tpu as pltpu
from jax.sharding import PartitionSpec as P

highest = lax.Precision.HIGHEST
SUB, LANE = 8, 128
ROWS = 31


def lane_pick(values, index):
    return jnp.take_along_axis(values, index, axis=1, mode="promise_in_bounds")


def stencil_kernel(counts_ref, table_ref, lists_ref, *refs):
    sources, (low_ref, top_ref, below_ref, picked_ref) = refs[:-4], refs[-4:]
    sub = lax.broadcasted_iota(jnp.int32, (SUB, LANE), 0)
    lane = lax.broadcasted_iota(jnp.int32, (SUB, LANE), 1)
    inner = sub < SUB - 1
    ids = []
    for layer in range(2):
        behind = jnp.broadcast_to(lists_ref[2, layer, :, 0:1], (SUB, LANE))
        behind = jnp.max(jnp.where(lane == sub, behind, -1), axis=0, keepdims=True)
        behind = jnp.broadcast_to(behind, (SUB, LANE))
        behind = jnp.where(lane < SUB - 1, behind, -1)
        ids.append(jnp.where(inner, lists_ref[0, layer], behind))
    picked_ref[...] = jnp.zeros(picked_ref.shape, jnp.float32)
    parts = 4
    for part in range(parts):
        owner = lax.rem(lax.axis_index("dom") + (parts - part), parts)
        count = counts_ref[0, owner]
        start = jnp.int32(0)
        for other in range(parts):
            start = start + jnp.where(owner > other, counts_ref[0, other], 0)
        group_of, lane_of = [], []
        for layer in range(2):
            place = ids[layer] - start
            held = (place >= 0) & (place < count)
            group_of.append(jnp.where(held, place >> 7, -1))
            lane_of.append(jnp.where(held, place & (LANE - 1), 0))
        halves = ((0,), (1,), (2, 3), (4,))[part]

        def pick_groups(step, carry):
            for unit in range(2):
                group = step * 2 + unit
                span = pl.ds(pl.multiple_of(group * LANE, LANE), LANE)
                here = [group_of[layer] == group for layer in range(2)]
                for row in range(ROWS):
                    half, line = divmod(row, 16) if len(halves) == 2 else (0, row)
                    source = sources[halves[half]]
                    line = jnp.broadcast_to(source[line : line + 1, span], (SUB, LANE))
                    for layer in range(2):
                        got = lane_pick(line, lane_of[layer])
                        picked_ref[layer, row] = jnp.where(here[layer], got, picked_ref[layer, row])
            return carry

        lax.fori_loop(0, (count + 2 * LANE - 1) // (2 * LANE), pick_groups, 0)
    low_ref[...] = jnp.zeros(low_ref.shape, jnp.float32)
    top_ref[...] = jnp.zeros(top_ref.shape, jnp.float32)
    below_ref[...] = jnp.zeros(below_ref.shape, jnp.float32)
    first_lane = lane == 0

    def from_behind(rows):
        edge = lane_pick(jnp.broadcast_to(rows[SUB - 1 : SUB], (SUB, LANE)), sub)
        return jnp.where(first_lane, edge, pltpu.roll(rows, 1, axis=1))

    for layer in range(2):
        grade = picked_ref[layer, 30]
        scale = jnp.zeros((SUB, LANE), jnp.float32)
        for level in range(table_ref.shape[0]):
            scale = jnp.where(grade == float(level), table_ref[level], scale)
        own = [picked_ref[layer, row] for row in range(24)]
        own += [picked_ref[layer, 24 + row] * scale for row in range(6)]
        behind = [from_behind(rows) for rows in own]
        for slot in range(4):
            data = own if slot < 2 else behind
            stress = [jnp.where(inner, data[24 + row], 0.0) for row in range(6)]
            grad = data[:24]
            if slot % 2 == 1:
                stress = [pltpu.roll(rows, 1, axis=0) for rows in stress]
                grad = [pltpu.roll(rows, 1, axis=0) for rows in grad]
            order = ((0, 5, 4), (5, 1, 3), (4, 3, 2))
            for corner in range(8):
                pushed = [
                    stress[order[i][0]] * grad[corner]
                    + stress[order[i][1]] * grad[8 + corner]
                    + stress[order[i][2]] * grad[16 + corner]
                    for i in range(3)
                ]
                offset = (corner % 2 - slot % 2 + 1) + 3 * (corner // 2 % 2 - slot // 2 + 1)
                offset += 9 * (corner // 4)
                upper = sum(grad[8 * i + slot + 4] * pushed[i] for i in range(3))
                lower = sum(grad[8 * i + slot] * pushed[i] for i in range(3))
                if layer == 0:
                    low_ref[offset] += upper
                    below_ref[offset] += lower
                else:
                    top_ref[offset] += upper
                    low_ref[offset + 9] += lower
    for ref in (low_ref, top_ref, below_ref):
        for offset in range(ref.shape[0]):
            if offset % 3 != 1:
                ref[offset] = pltpu.roll(ref[offset], (offset % 3 - 1) % SUB, axis=0)


def local_stencils(counts, table, lists, sources):
    vmem = pl.BlockSpec(memory_space=pltpu.VMEM)
    smem = pl.BlockSpec(memory_space=pltpu.SMEM)
    return pl.pallas_call(
        stencil_kernel,
        out_shape=[
            jax.ShapeDtypeStruct((27, SUB, LANE), jnp.float32),
            jax.ShapeDtypeStruct((18, SUB, LANE), jnp.float32),
            jax.ShapeDtypeStruct((18, SUB, LANE), jnp.float32),
        ],
        in_specs=[smem, smem] + [vmem] * (1 + len(sources)),
        out_specs=[vmem, vmem, vmem],
        scratch_shapes=[pltpu.VMEM((2, ROWS, SUB, LANE), jnp.float32)],
        compiler_params=pltpu.CompilerParams(vmem_limit_bytes=24 * 1024 * 1024),
    )(counts, table, lists, *sources)


def split_kernel(start_ref, diag_ref, slab_ref, edges_ref):
    comps, vecs = start_ref.shape[:2]
    total = comps * vecs
    lane = lax.broadcasted_iota(jnp.int32, (SUB, LANE), 1)
    found = [jnp.zeros((SUB, LANE), jnp.float32)] * 4
    for comp in range(comps):
        for floor in range(2):
            slab_ref[2 * total + 2 * comp + floor] = diag_ref[comp, floor]

        def step(vec, carry):
            out = []
            place = comp * vecs + vec
            for floor in range(2):
                rows = start_ref[comp, vec, floor]
                slab_ref[floor * total + place] = rows
                out.append(jnp.where(lane == place, pltpu.roll(rows, place, axis=1), carry[floor]))
            for floor in range(2):
                rows = start_ref[comp, vec, floor]
                turned = pltpu.roll(rows, place + 1, axis=1)
                out.append(jnp.where(lane == place, turned, carry[2 + floor]))
            return tuple(out)

        found = lax.fori_loop(0, vecs, step, tuple(found), unroll=16)
    for k in range(4):
        edges_ref[k] = found[k]


def split_slab(start_block, diagonal):
    total = start_block.shape[0] * start_block.shape[1]
    return call_whole(
        split_kernel,
        [
            jax.ShapeDtypeStruct((2 * total + 2 * start_block.shape[0], SUB, LANE), jnp.float32),
            jax.ShapeDtypeStruct((4, SUB, LANE), jnp.float32),
        ],
        start_block, diagonal,
    )


def operator_rows(floors, behind, ahead, taps, weights, outs, edges, total, vecs, width):
    lane = lax.broadcasted_iota(jnp.int32, (SUB, LANE), 1)

    def step(index, carry):
        first = index * width
        rows = []
        for unit in range(width):
            vec = first + unit
            for z, (ref, base) in enumerate(floors):
                mid = ref[base + vec]
                left = pltpu.roll(behind[z], LANE - vec, axis=1)
                left = jnp.where(lane == 0, left, pltpu.roll(mid, 1, axis=1))
                right = pltpu.roll(ahead[z], LANE - 1 - vec, axis=1)
                right = jnp.where(lane == LANE - 1, right, pltpu.roll(mid, LANE - 1, axis=1))
                rows.append((left, mid, right))
        new = list(carry)
        comp = first // vecs
        for floor, (out_ref, base) in enumerate(outs):
            weight = weights[floor](comp)
            sums = [[None] * 3 for _ in range(width)]
            for offset in range(27):
                tap = taps[floor][offset]
                dx, dy, dz = offset % 3, offset // 3 % 3, offset // 9
                for unit in range(width):
                    term = tap * rows[len(floors) * unit + floor + dz][dy]
                    old = sums[unit][dx]
                    sums[unit][dx] = term if old is None else old + term
            for unit in range(width):
                vec = first + unit
                result = weight * rows[len(floors) * unit + floor + 1][1] + sums[unit][1]
                result = result + pltpu.roll(sums[unit][0], 1, axis=0)
                result = result + pltpu.roll(sums[unit][2], SUB - 1, axis=0)
                out_ref[base + vec] = result
                if edges is not None:
                    for side in range(2):
                        turned = pltpu.roll(result, vec + side, axis=1)
                        spot = 2 * floor + side
                        new[spot] = jnp.where(lane == vec, turned, new[spot])
        return tuple(new)

    zero = jnp.zeros((SUB, LANE), jnp.float32)
    count = 0 if edges is None else 2 * len(outs)
    done = lax.fori_loop(0, total // width, step, (zero,) * count)
    if edges is not None:
        for floor in range(len(outs)):
            edges[0][floor] = done[2 * floor]
            edges[1][floor] = done[2 * floor + 1]


def first_operator_kernel(
    under_ref, own_ref, over_ref, low_ref, top_ref, below_ref, from_above_ref, from_below_ref,
    columns_ref, image_ref, left_ref, right_ref, high_ref, under_taps_ref,
):
    total = image_ref.shape[0] // 4
    comps = (own_ref.shape[0] - 2 * total) // 2
    diag_row = 2 * total
    inside = jnp.where(lax.axis_index("slab") > 0, 1.0, 0.0)
    cols_refs = ((from_below_ref, 18), (columns_ref, 0), (from_above_ref, 45))
    high_ref[0:18] = top_ref[...]
    high_ref[18:27] = from_above_ref[36:45]
    high_ref[9:18] = high_ref[9:18] + from_above_ref[27:36]
    under_taps_ref[0:9] = from_below_ref[0:9] * inside
    under_taps_ref[9:18] = (from_below_ref[9:18] + below_ref[0:9]) * inside
    under_taps_ref[18:27] = below_ref[9:18] * inside
    slabs = (under_ref, own_ref, over_ref)
    floors = [(ref, floor * total) for ref in slabs for floor in range(2)]
    behind = [ref[row + floor] for ref, row in cols_refs for floor in range(2)]
    ahead = [ref[row + 2 + floor] for ref, row in cols_refs for floor in range(2)]

    def weight(ref, floor):
        return lambda comp: ref[diag_row + 2 * comp + floor]

    operator_rows(
        floors, behind, ahead, (under_taps_ref, low_ref, high_ref, from_above_ref),
        (weight(under_ref, 1), weight(own_ref, 0), weight(own_ref, 1), weight(over_ref, 0)),
        [(image_ref, floor * total) for floor in range(4)],
        (left_ref, right_ref), total, total // comps, 8,
    )


def second_operator_kernel(
    image_ref, from_left_ref, from_right_ref, low_ref, high_ref, diag_ref, out_ref, gram_ref
):
    total = out_ref.shape[0] // 2
    comps = diag_ref.shape[0]
    vecs = total // comps

    def weight(floor):
        return lambda comp: diag_ref[comp, floor]

    operator_rows(
        [(image_ref, floor * total) for floor in range(4)],
        [from_left_ref[floor] for floor in range(4)],
        [from_right_ref[floor] for floor in range(4)],
        (low_ref, high_ref), (weight(0), weight(1)),
        [(out_ref, floor * total) for floor in range(2)],
        None, total, vecs, 16,
    )
    blocks = [
        ((image_ref, (1 + floor) * total), (out_ref, floor * total)) for floor in range(2)
    ]
    gram_ref[...] = local_gram(blocks, comps, vecs, vecs)


def paired_rows(parts, start, vecs, across):
    rows = []
    for ref, base in parts:
        span = pl.ds(base + start, vecs)
        rows.append(jnp.concatenate([ref[span, across, :], ref[span, across + 1, :]], axis=1))
    return jnp.concatenate(rows, axis=0)


def local_gram(blocks, comps, vecs, skipped):
    gram = None
    for comp in range(comps):
        for parts in blocks:
            for across in range(0, SUB, 2):
                rows = paired_rows(parts, comp * vecs, vecs, across)
                term = dot_both(rows, rows[skipped:])
                gram = term if gram is None else gram + term
    return gram


def first_gram_kernel(own_ref, image_ref, gram_ref):
    vecs = gram_ref.shape[0] // 2
    total = image_ref.shape[0] // 4
    blocks = [
        ((own_ref, floor * total), (image_ref, (1 + floor) * total)) for floor in range(2)
    ]
    gram_ref[...] = local_gram(blocks, total // vecs, vecs, 0)


def call_whole(kernel, out_shape, *operands, scratch_shapes=()):
    vmem = pl.BlockSpec(memory_space=pltpu.VMEM)
    return pl.pallas_call(
        kernel,
        out_shape=out_shape,
        in_specs=[vmem] * len(operands),
        out_specs=[vmem] * len(out_shape),
        scratch_shapes=scratch_shapes,
        compiler_params=pltpu.CompilerParams(vmem_limit_bytes=32 * 1024 * 1024),
    )(*operands)


def apply_first(under, own, over, low, top, below, from_above, from_below, columns, total):
    edge = jax.ShapeDtypeStruct((4, SUB, LANE), jnp.float32)
    taps = jax.ShapeDtypeStruct((27, SUB, LANE), jnp.float32)
    return call_whole(
        first_operator_kernel,
        [jax.ShapeDtypeStruct((4 * total, SUB, LANE), jnp.float32), edge, edge, taps],
        under, own, over, low, top, below, from_above, from_below, columns,
        scratch_shapes=[pltpu.VMEM((27, SUB, LANE), jnp.float32)],
    )


def apply_second(image, from_left, from_right, low, high, diagonal):
    total = image.shape[0] // 4
    vecs = total // diagonal.shape[0]
    return call_whole(
        second_operator_kernel,
        [
            jax.ShapeDtypeStruct((2 * total, SUB, LANE), jnp.float32),
            jax.ShapeDtypeStruct((2 * vecs, vecs), jnp.float32),
        ],
        image, from_left, from_right, low, high, diagonal,
    )


def first_gram(own, image, vecs):
    shape = jax.ShapeDtypeStruct((2 * vecs, 2 * vecs), jnp.float32)
    return call_whole(first_gram_kernel, [shape], own, image)[0]


def dot_rows(left, right):
    return lax.dot_general(
        left, right, (((1,), (0,)), ((), ())), precision=highest, preferred_element_type=jnp.float32
    )


def dot_both(left, right):
    return lax.dot_general(
        left, right, (((1,), (1,)), ((), ())), precision=highest, preferred_element_type=jnp.float32
    )


def eliminate(gram):
    size = gram.shape[0]
    row_id = lax.broadcasted_iota(jnp.int32, (size, 2 * size), 0)
    lane_id = lax.broadcasted_iota(jnp.int32, (size, 2 * size), 1)
    identity = (row_id[:, :size] == lane_id[:, :size]).astype(jnp.float32)
    work = jnp.concatenate([gram, identity], axis=1)
    panel = 8
    for first in range(0, size, panel):
        spots = range(first, first + panel)
        columns = [jnp.broadcast_to(work[:, k : k + 1], (size, 2 * size)) for k in spots]
        rows = [work[k : k + 1, :] for k in spots]
        for j, k in enumerate(spots):
            pivot = columns[j][k : k + 1, :]
            inverse = lax.rsqrt(pivot)
            inverse = inverse * (1.5 - 0.5 * pivot * inverse * inverse)
            rows[j] = rows[j] * inverse
            columns[j] = columns[j] * inverse
            for later in range(j + 1, panel):
                weight = columns[j][first + later : first + later + 1, :]
                columns[later] = columns[later] - columns[j] * weight
                rows[later] = rows[later] - rows[j] * weight
        reduced = work
        for j in range(panel):
            reduced = reduced - columns[j] * rows[j]
        work = jnp.where(row_id >= first + panel, reduced, work)
        for j, k in enumerate(spots):
            work = jnp.where(row_id == k, rows[j], work)
    upper = jnp.where(row_id[:, :size] <= lane_id[:, :size], work[:, :size], 0.0)
    return upper, work[:, size:]


def finish_kernel(gram_ref, own_ref, image_ref, second_ref, next_ref, diag_ref, offdiag_ref):
    total = image_ref.shape[0] // 4
    vecs = diag_ref.shape[1]
    comps = next_ref.shape[0]
    zero = jnp.zeros((vecs, vecs), jnp.float32)
    eye = (
        lax.broadcasted_iota(jnp.int32, (vecs, vecs), 0)
        == lax.broadcasted_iota(jnp.int32, (vecs, vecs), 1)
    ).astype(jnp.float32)

    def grid(rows):
        return jnp.concatenate([jnp.concatenate(row, axis=1) for row in rows], axis=0)

    def block(matrix, row, column):
        return matrix[row * vecs : (row + 1) * vecs, column * vecs : (column + 1) * vecs]

    packed = gram_ref[...]
    moments = [packed[:vecs, k * vecs : (k + 1) * vecs] for k in range(4)]
    moments.append(
        jnp.concatenate([packed[vecs:, k * vecs : (k + 1) * vecs] for k in range(4)], axis=0)
    )
    gram = grid([moments[k : k + 3] for k in range(3)])
    upper_0, inverse_0 = eliminate(block(gram, 0, 0))
    spread = grid([[inverse_0, zero, zero], [zero, inverse_0, zero], [zero, zero, inverse_0]])
    krylov = dot_both(dot_rows(spread, gram), spread)
    alpha_1, alpha_1_t = block(krylov, 0, 1), block(krylov, 1, 0)
    change = grid([[eye, zero, zero], [-alpha_1_t, eye, zero], [zero, -alpha_1_t, eye]])
    moved = dot_both(dot_rows(change, krylov), change)
    upper_1, inverse_1 = eliminate(block(moved, 1, 1))
    second = grid([[zero, inverse_1, zero], [-upper_1, zero, inverse_1]])
    products = dot_both(dot_rows(second, moved), second)
    alpha_2, alpha_2_t = block(products, 0, 1), block(products, 1, 0)
    upper_2, inverse_2 = eliminate(block(products, 1, 1) - dot_rows(alpha_2_t, alpha_2))
    residual = jnp.concatenate([-upper_1, -dot_rows(alpha_2_t, inverse_1), inverse_1], axis=1)
    coefs = dot_rows(dot_rows(dot_rows(inverse_2, residual), change), spread)
    diag_ref[0] = alpha_1
    diag_ref[1] = alpha_2
    offdiag_ref[0] = upper_0
    offdiag_ref[1] = upper_1
    offdiag_ref[2] = upper_2
    for comp in range(comps):
        for floor in range(2):
            parts = (
                (own_ref, floor * total),
                (image_ref, (1 + floor) * total),
                (second_ref, floor * total),
            )
            for across in range(0, SUB, 2):
                mixed = dot_rows(coefs, paired_rows(parts, comp * vecs, vecs, across))
                next_ref[comp, :, floor, across, :] = mixed[:, :LANE]
                next_ref[comp, :, floor, across + 1, :] = mixed[:, LANE:]


def finish(gram, blocks, out_shape, vecs):
    return call_whole(
        finish_kernel,
        [
            jax.ShapeDtypeStruct(out_shape, jnp.float32),
            jax.ShapeDtypeStruct((2, vecs, vecs), jnp.float32),
            jax.ShapeDtypeStruct((3, vecs, vecs), jnp.float32),
        ],
        gram, *blocks,
    )


def exchange(value, axis, route):
    size = lax.axis_size(axis)
    return lax.ppermute(value, axis, [(i, route(i)) for i in range(size)])


def ring_pairs(stride, size, odd_first):
    def route(i):
        digit = i // stride % size
        if odd_first:
            partner = (digit + 1) % size if digit % 2 == 0 else (digit - 1) % size
        else:
            partner = (digit + 1) % size if digit % 2 == 1 else (digit - 1) % size
        return i + (partner - digit) * stride

    return route


def far_pairs(stride):
    partners = (3, 6, 5, 0, 7, 2, 1, 4)

    def route(i):
        digit = i // stride % 8
        return i + (partners[digit] - digit) * stride

    return route


def mesh_sum(value):
    steps = [
        ("slab", ring_pairs(1, 2, True)),
        ("dom", ring_pairs(1, 4, True)),
        ("dom", ring_pairs(1, 4, False)),
        ("slab", ring_pairs(2, 4, True)),
        ("slab", ring_pairs(2, 4, False)),
        ("slab", ring_pairs(8, 8, True)),
        ("slab", ring_pairs(8, 8, False)),
        ("slab", far_pairs(8)),
    ]
    for axis, route in steps:
        value = value + exchange(value, axis, route)
    return value


def shifted(value, axis, steps, wrap):
    size = lax.axis_size(axis)
    route = [(i, (i + steps) % size) for i in range(size) if wrap or 0 <= i + steps < size]
    return lax.ppermute(value, axis, route)


def gathered(elem_grad, elem_stress, elem_grade):
    capacity = elem_grad.shape[2]
    packed = jnp.concatenate(
        [
            elem_grad.reshape(24, capacity),
            elem_stress,
            elem_grade.astype(jnp.float32)[None],
            jnp.zeros((1, capacity), jnp.float32),
        ],
        axis=0,
    )
    ahead, behind = shifted(packed, "dom", 1, True), shifted(packed, "dom", -1, True)
    low, high = shifted(ahead[:16], "dom", 1, True), shifted(behind[16:], "dom", -1, True)
    return [packed, ahead, low, high, behind]


def per_device(
    elem_grad,
    elem_stress,
    elem_grade,
    grade_scale,
    part_counts,
    node_lists,
    stiff_diag,
    start_block,
):
    comps, vecs = start_block.shape[:2]
    total = comps * vecs
    own, edges = split_slab(start_block, stiff_diag)
    sources = gathered(elem_grad, elem_stress, elem_grade)
    from_left = shifted(edges[2:], "dom", 1, True)
    from_right = shifted(edges[:2], "dom", -1, True)
    columns = jnp.concatenate([from_left, from_right], axis=0)
    under = shifted(own, "slab", 1, False)
    over = shifted(own, "slab", -1, False)
    sources, under, over = lax.optimization_barrier((sources, under, over))
    low, top, below = local_stencils(part_counts, grade_scale, node_lists, sources)
    from_above = shifted(jnp.concatenate([low, below, columns], axis=0), "slab", -1, False)
    from_below = shifted(jnp.concatenate([top, columns], axis=0), "slab", 1, False)
    image, left, right, high = apply_first(
        under, own, over, low, top, below, from_above, from_below, columns, total
    )
    from_left = shifted(right, "dom", 1, True)
    from_right = shifted(left, "dom", -1, True)
    outer = first_gram(own, image, vecs)
    second, inner = apply_second(image, from_left, from_right, low, high, stiff_diag)
    last = inner[vecs:]
    packed = jnp.concatenate(
        [
            jnp.concatenate([outer[:vecs], outer[vecs:, vecs:], inner[:vecs]], axis=1),
            jnp.concatenate([last[k * 8 : k * 8 + 8] for k in range(vecs // 8)], axis=1),
        ],
        axis=0,
    )
    dof_count = (
        start_block.size // vecs * lax.axis_size("slab") * lax.axis_size("dom")
    )
    packed = mesh_sum(packed) / dof_count
    return finish(packed, (own, image, second), start_block.shape, vecs)


def solution(mesh):
    in_specs = (
        P(None, None, ("slab", "dom")),
        P(None, ("slab", "dom")),
        P(("slab", "dom")),
        P(),
        P("slab", None),
        P(None, "slab", None, "dom"),
        P(None, "slab", None, "dom"),
        P(None, None, "slab", None, "dom"),
    )
    out_specs = (P(None, None, "slab", None, "dom"), P(), P())
    return jax.shard_map(
        per_device, mesh=mesh, in_specs=in_specs, out_specs=out_specs, check_vma=False
    )
```

```python
import jax
import jax.numpy as jnp
from jax import lax
from jax.experimental import pallas as pl
from jax.experimental.pallas import tpu as pltpu
from jax.sharding import Mesh
from jax.sharding import PartitionSpec as P

highest = lax.Precision.HIGHEST
SUB, LANE = 8, 128
ROWS = 31
UNITS = 3
SLAB = ("z", "x", "core")


def lane_pick(values, index):
    return jnp.take_along_axis(values, index, axis=1, mode="promise_in_bounds")


def stencil_kernel(counts_ref, table_ref, lists_ref, *refs):
    sources, (low_ref, top_ref, below_ref, picked_ref) = refs[:-4], refs[-4:]
    sub = lax.broadcasted_iota(jnp.int32, (SUB, LANE), 0)
    lane = lax.broadcasted_iota(jnp.int32, (SUB, LANE), 1)
    inner = sub < SUB - 1
    ids = []
    for layer in range(2):
        behind = jnp.broadcast_to(lists_ref[2, layer, :, 0:1], (SUB, LANE))
        behind = jnp.max(jnp.where(lane == sub, behind, -1), axis=0, keepdims=True)
        behind = jnp.broadcast_to(behind, (SUB, LANE))
        behind = jnp.where(lane < SUB - 1, behind, -1)
        ids.append(jnp.where(inner, lists_ref[0, layer], behind))
    picked_ref[...] = jnp.zeros(picked_ref.shape, jnp.float32)
    parts = 4
    for part in range(parts):
        owner = lax.rem(lax.axis_index("dom") + (parts - part), parts)
        count = counts_ref[0, owner]
        start = jnp.int32(0)
        for other in range(parts):
            start = start + jnp.where(owner > other, counts_ref[0, other], 0)
        group_of, lane_of = [], []
        for layer in range(2):
            place = ids[layer] - start
            held = (place >= 0) & (place < count)
            group_of.append(jnp.where(held, place >> 7, -1))
            lane_of.append(jnp.where(held, place & (LANE - 1), 0))
        halves = ((0,), (1,), (2, 3), (4,))[part]

        def pick_groups(step, carry):
            spans, here = [], []
            for unit in range(UNITS):
                group = step * UNITS + unit
                spans.append(pl.ds(pl.multiple_of(group * LANE, LANE), LANE))
                here.append([group_of[layer] == group for layer in range(2)])
            for row in range(ROWS):
                half, line = divmod(row, 16) if len(halves) == 2 else (0, row)
                source = sources[halves[half]]
                found = [picked_ref[layer, row] for layer in range(2)]
                for unit in range(UNITS):
                    values = jnp.broadcast_to(source[line : line + 1, spans[unit]], (SUB, LANE))
                    for layer in range(2):
                        got = lane_pick(values, lane_of[layer])
                        found[layer] = jnp.where(here[unit][layer], got, found[layer])
                for layer in range(2):
                    picked_ref[layer, row] = found[layer]
            return carry

        width = UNITS * LANE
        lax.fori_loop(0, (count + width - 1) // width, pick_groups, 0)
    low_ref[...] = jnp.zeros(low_ref.shape, jnp.float32)
    top_ref[...] = jnp.zeros(top_ref.shape, jnp.float32)
    below_ref[...] = jnp.zeros(below_ref.shape, jnp.float32)
    first_lane = lane == 0

    def from_behind(rows):
        edge = lane_pick(jnp.broadcast_to(rows[SUB - 1 : SUB], (SUB, LANE)), sub)
        return jnp.where(first_lane, edge, pltpu.roll(rows, 1, axis=1))

    for layer in range(2):
        grade = picked_ref[layer, 30]
        scale = jnp.zeros((SUB, LANE), jnp.float32)
        for level in range(table_ref.shape[0]):
            scale = jnp.where(grade == float(level), table_ref[level], scale)
        own = [picked_ref[layer, row] for row in range(24)]
        own += [picked_ref[layer, 24 + row] * scale for row in range(6)]
        behind = [from_behind(rows) for rows in own]
        for slot in range(4):
            data = own if slot < 2 else behind
            stress = [jnp.where(inner, data[24 + row], 0.0) for row in range(6)]
            grad = data[:24]
            if slot % 2 == 1:
                stress = [pltpu.roll(rows, 1, axis=0) for rows in stress]
                grad = [pltpu.roll(rows, 1, axis=0) for rows in grad]
            order = ((0, 5, 4), (5, 1, 3), (4, 3, 2))
            for corner in range(8):
                pushed = [
                    stress[order[i][0]] * grad[corner]
                    + stress[order[i][1]] * grad[8 + corner]
                    + stress[order[i][2]] * grad[16 + corner]
                    for i in range(3)
                ]
                offset = (corner % 2 - slot % 2 + 1) + 3 * (corner // 2 % 2 - slot // 2 + 1)
                offset += 9 * (corner // 4)
                upper = sum(grad[8 * i + slot + 4] * pushed[i] for i in range(3))
                lower = sum(grad[8 * i + slot] * pushed[i] for i in range(3))
                if layer == 0:
                    low_ref[offset] += upper
                    below_ref[offset] += lower
                else:
                    top_ref[offset] += upper
                    low_ref[offset + 9] += lower
    for ref in (low_ref, top_ref, below_ref):
        for offset in range(ref.shape[0]):
            if offset % 3 != 1:
                ref[offset] = pltpu.roll(ref[offset], (offset % 3 - 1) % SUB, axis=0)


def local_stencils(counts, table, lists, sources):
    vmem = pl.BlockSpec(memory_space=pltpu.VMEM)
    smem = pl.BlockSpec(memory_space=pltpu.SMEM)
    return pl.pallas_call(
        stencil_kernel,
        out_shape=[
            jax.ShapeDtypeStruct((27, SUB, LANE), jnp.float32),
            jax.ShapeDtypeStruct((18, SUB, LANE), jnp.float32),
            jax.ShapeDtypeStruct((18, SUB, LANE), jnp.float32),
        ],
        in_specs=[smem, smem] + [vmem] * (1 + len(sources)),
        out_specs=[vmem, vmem, vmem],
        scratch_shapes=[pltpu.VMEM((2, ROWS, SUB, LANE), jnp.float32)],
        compiler_params=pltpu.CompilerParams(vmem_limit_bytes=24 * 1024 * 1024),
    )(counts, table, lists, *sources)


def split_kernel(start_ref, diag_ref, slab_ref, edges_ref):
    comps, vecs = start_ref.shape[:2]
    total = comps * vecs
    lane = lax.broadcasted_iota(jnp.int32, (SUB, LANE), 1)
    found = [jnp.zeros((SUB, LANE), jnp.float32)] * 4
    for comp in range(comps):
        for floor in range(2):
            slab_ref[2 * total + 2 * comp + floor] = diag_ref[comp, floor]

        def step(vec, carry):
            out = []
            place = comp * vecs + vec
            for floor in range(2):
                rows = start_ref[comp, vec, floor]
                slab_ref[floor * total + place] = rows
                out.append(jnp.where(lane == place, pltpu.roll(rows, place, axis=1), carry[floor]))
            for floor in range(2):
                rows = start_ref[comp, vec, floor]
                turned = pltpu.roll(rows, place + 1, axis=1)
                out.append(jnp.where(lane == place, turned, carry[2 + floor]))
            return tuple(out)

        found = lax.fori_loop(0, vecs, step, tuple(found), unroll=16)
    for k in range(4):
        edges_ref[k] = found[k]


def split_slab(start_block, diagonal):
    total = start_block.shape[0] * start_block.shape[1]
    return call_whole(
        split_kernel,
        [
            jax.ShapeDtypeStruct((2 * total + 2 * start_block.shape[0], SUB, LANE), jnp.float32),
            jax.ShapeDtypeStruct((4, SUB, LANE), jnp.float32),
        ],
        start_block, diagonal,
    )


def operator_rows(floors, behind, ahead, taps, weights, outs, edges, total, vecs, width):
    lane = lax.broadcasted_iota(jnp.int32, (SUB, LANE), 1)

    def step(index, carry):
        first = index * width
        rows = []
        for unit in range(width):
            vec = first + unit
            for z, (ref, base) in enumerate(floors):
                mid = ref[base + vec]
                left = pltpu.roll(behind[z], LANE - vec, axis=1)
                left = jnp.where(lane == 0, left, pltpu.roll(mid, 1, axis=1))
                right = pltpu.roll(ahead[z], LANE - 1 - vec, axis=1)
                right = jnp.where(lane == LANE - 1, right, pltpu.roll(mid, LANE - 1, axis=1))
                rows.append((left, mid, right))
        new = list(carry)
        comp = first // vecs
        for floor, (out_ref, base) in enumerate(outs):
            weight = weights[floor](comp)
            sums = [[None] * 3 for _ in range(width)]
            for offset in range(27):
                tap = taps[floor][offset]
                dx, dy, dz = offset % 3, offset // 3 % 3, offset // 9
                for unit in range(width):
                    term = tap * rows[len(floors) * unit + floor + dz][dy]
                    old = sums[unit][dx]
                    sums[unit][dx] = term if old is None else old + term
            for unit in range(width):
                vec = first + unit
                result = weight * rows[len(floors) * unit + floor + 1][1] + sums[unit][1]
                result = result + pltpu.roll(sums[unit][0], 1, axis=0)
                result = result + pltpu.roll(sums[unit][2], SUB - 1, axis=0)
                out_ref[base + vec] = result
                if edges is not None:
                    for side in range(2):
                        turned = pltpu.roll(result, vec + side, axis=1)
                        spot = 2 * floor + side
                        new[spot] = jnp.where(lane == vec, turned, new[spot])
        return tuple(new)

    zero = jnp.zeros((SUB, LANE), jnp.float32)
    count = 0 if edges is None else 2 * len(outs)
    done = lax.fori_loop(0, total // width, step, (zero,) * count)
    if edges is not None:
        for floor in range(len(outs)):
            edges[0][floor] = done[2 * floor]
            edges[1][floor] = done[2 * floor + 1]


def first_operator_kernel(
    under_ref, own_ref, over_ref, low_ref, top_ref, below_ref, from_above_ref, from_below_ref,
    columns_ref, image_ref, left_ref, right_ref, high_ref, under_taps_ref,
):
    total = image_ref.shape[0] // 4
    comps = (own_ref.shape[0] - 2 * total) // 2
    diag_row = 2 * total
    inside = jnp.where(sum(lax.axis_index(name) for name in SLAB) > 0, 1.0, 0.0)
    cols_refs = ((from_below_ref, 18), (columns_ref, 0), (from_above_ref, 45))
    high_ref[0:18] = top_ref[...]
    high_ref[18:27] = from_above_ref[36:45]
    high_ref[9:18] = high_ref[9:18] + from_above_ref[27:36]
    under_taps_ref[0:9] = from_below_ref[0:9] * inside
    under_taps_ref[9:18] = (from_below_ref[9:18] + below_ref[0:9]) * inside
    under_taps_ref[18:27] = below_ref[9:18] * inside
    slabs = (under_ref, own_ref, over_ref)
    floors = [(ref, floor * total) for ref in slabs for floor in range(2)]
    behind = [ref[row + floor] for ref, row in cols_refs for floor in range(2)]
    ahead = [ref[row + 2 + floor] for ref, row in cols_refs for floor in range(2)]

    def weight(ref, floor):
        return lambda comp: ref[diag_row + 2 * comp + floor]

    operator_rows(
        floors, behind, ahead, (under_taps_ref, low_ref, high_ref, from_above_ref),
        (weight(under_ref, 1), weight(own_ref, 0), weight(own_ref, 1), weight(over_ref, 0)),
        [(image_ref, floor * total) for floor in range(4)],
        (left_ref, right_ref), total, total // comps, 8,
    )


def second_operator_kernel(
    image_ref, from_left_ref, from_right_ref, low_ref, high_ref, diag_ref, moment_ref, outer_ref,
    out_ref, packed_ref,
):
    total = out_ref.shape[0] // 2
    comps = diag_ref.shape[0]
    vecs = total // comps

    def weight(floor):
        return lambda comp: diag_ref[comp, floor]

    operator_rows(
        [(image_ref, floor * total) for floor in range(4)],
        [from_left_ref[floor] for floor in range(4)],
        [from_right_ref[floor] for floor in range(4)],
        (low_ref, high_ref), (weight(0), weight(1)),
        [(out_ref, floor * total) for floor in range(2)],
        None, total, vecs, 16,
    )
    blocks = [
        ((image_ref, (1 + floor) * total), (out_ref, floor * total)) for floor in range(2)
    ]
    inner = local_gram(blocks, comps, vecs, vecs)
    outer = outer_ref[...]
    pack_moments(
        packed_ref, moment_ref[...], outer[:vecs], outer[vecs:], inner[:vecs], inner[vecs:]
    )


def square_ids(size):
    return (
        lax.broadcasted_iota(jnp.int32, (size, size), 0),
        lax.broadcasted_iota(jnp.int32, (size, size), 1),
    )


def pack_moments(packed_ref, *moments):
    size = moments[0].shape[0]
    half = size // 2
    row, column = square_ids(size)
    squares = [
        jnp.where(row <= column, moments[0], moments[1]),
        jnp.where(row <= column, moments[2], moments[3]),
    ]
    extra = jnp.zeros((size, size), jnp.float32)
    for k in range(2):
        line = jnp.sum(jnp.where(row == column, moments[2 * k + 1], 0.0), axis=0, keepdims=True)
        turned = jnp.concatenate([line[:, half:], line[:, :half]], axis=1)
        extra = jnp.where(row == half + 2 * k, line, extra)
        extra = jnp.where(row == half + 2 * k + 1, turned, extra)
    squares.append(jnp.where(row <= column, moments[4], extra))
    for k, square in enumerate(squares):
        packed_ref[SUB * k : SUB * (k + 1)] = jnp.concatenate(
            [square[SUB * part : SUB * (part + 1)] for part in range(size // SUB)], axis=1
        )


def unpack_moments(packed, size):
    half = size // 2
    row, column = square_ids(size)
    squares = [
        jnp.concatenate(
            [
                packed[SUB * k : SUB * (k + 1), size * part : size * (part + 1)]
                for part in range(size // SUB)
            ],
            axis=0,
        )
        for k in range(3)
    ]
    flipped = dot_both((row == column).astype(jnp.float32), jnp.concatenate(squares, axis=0))
    moments = []
    for k, square in enumerate(squares):
        mirror = flipped[:, size * k : size * (k + 1)]
        moments.append(jnp.where(row <= column, square, mirror))
        if k < 2:
            spot = half + 2 * k
            line = jnp.concatenate(
                [squares[2][spot : spot + 1, :half], squares[2][spot + 1 : spot + 2, :half]],
                axis=1,
            )
            lower = jnp.where(row > column, square, mirror)
            moments.append(jnp.where(row == column, line, lower))
    return moments


def paired_rows(parts, start, vecs, across):
    rows = []
    for ref, base in parts:
        span = pl.ds(base + start, vecs)
        rows.append(jnp.concatenate([ref[span, across, :], ref[span, across + 1, :]], axis=1))
    return jnp.concatenate(rows, axis=0)


def local_gram(blocks, comps, vecs, skipped):
    gram = None
    for comp in range(comps):
        for parts in blocks:
            for across in range(0, SUB, 2):
                rows = paired_rows(parts, comp * vecs, vecs, across)
                term = dot_both(rows, rows[skipped:])
                gram = term if gram is None else gram + term
    return gram


def start_gram_kernel(own_ref, gram_ref):
    vecs = gram_ref.shape[0]
    total = own_ref.shape[0] * vecs // (2 * vecs + 2)
    blocks = [((own_ref, floor * total),) for floor in range(2)]
    gram_ref[...] = local_gram(blocks, total // vecs, vecs, 0)


def first_gram_kernel(own_ref, image_ref, gram_ref):
    vecs = gram_ref.shape[1]
    total = image_ref.shape[0] // 4
    blocks = [
        ((own_ref, floor * total), (image_ref, (1 + floor) * total)) for floor in range(2)
    ]
    gram_ref[...] = local_gram(blocks, total // vecs, vecs, vecs)


def call_whole(kernel, out_shape, *operands, scratch_shapes=()):
    vmem = pl.BlockSpec(memory_space=pltpu.VMEM)
    return pl.pallas_call(
        kernel,
        out_shape=out_shape,
        in_specs=[vmem] * len(operands),
        out_specs=[vmem] * len(out_shape),
        scratch_shapes=scratch_shapes,
        compiler_params=pltpu.CompilerParams(vmem_limit_bytes=32 * 1024 * 1024),
    )(*operands)


def apply_first(under, own, over, low, top, below, from_above, from_below, columns, total):
    edge = jax.ShapeDtypeStruct((4, SUB, LANE), jnp.float32)
    taps = jax.ShapeDtypeStruct((27, SUB, LANE), jnp.float32)
    return call_whole(
        first_operator_kernel,
        [jax.ShapeDtypeStruct((4 * total, SUB, LANE), jnp.float32), edge, edge, taps],
        under, own, over, low, top, below, from_above, from_below, columns,
        scratch_shapes=[pltpu.VMEM((27, SUB, LANE), jnp.float32)],
    )


def apply_second(image, from_left, from_right, low, high, diagonal, moment, outer):
    total = image.shape[0] // 4
    vecs = total // diagonal.shape[0]
    return call_whole(
        second_operator_kernel,
        [
            jax.ShapeDtypeStruct((2 * total, SUB, LANE), jnp.float32),
            jax.ShapeDtypeStruct((3 * SUB, SUB * vecs // 2), jnp.float32),
        ],
        image, from_left, from_right, low, high, diagonal, moment, outer,
    )


def start_gram(own, vecs):
    return call_whole(start_gram_kernel, [jax.ShapeDtypeStruct((vecs, vecs), jnp.float32)], own)[0]


def first_gram(own, image, vecs):
    shape = jax.ShapeDtypeStruct((2 * vecs, vecs), jnp.float32)
    return call_whole(first_gram_kernel, [shape], own, image)[0]


def dot_rows(left, right):
    return lax.dot_general(
        left, right, (((1,), (0,)), ((), ())), precision=highest, preferred_element_type=jnp.float32
    )


def dot_both(left, right):
    return lax.dot_general(
        left, right, (((1,), (1,)), ((), ())), precision=highest, preferred_element_type=jnp.float32
    )


def eliminate(gram):
    size = gram.shape[0]
    row_id = lax.broadcasted_iota(jnp.int32, (size, 2 * size), 0)
    lane_id = lax.broadcasted_iota(jnp.int32, (size, 2 * size), 1)
    identity = (row_id[:, :size] == lane_id[:, :size]).astype(jnp.float32)
    work = jnp.concatenate([gram, identity], axis=1)
    panel = 16
    for first in range(0, size, panel):
        spots = range(first, first + panel)
        columns = [jnp.broadcast_to(work[:, k : k + 1], (size, 2 * size)) for k in spots]
        rows = [work[k : k + 1, :] for k in spots]
        for j, k in enumerate(spots):
            pivot = columns[j][k : k + 1, :]
            inverse = lax.rsqrt(pivot)
            inverse = inverse * (1.5 - 0.5 * pivot * inverse * inverse)
            rows[j] = rows[j] * inverse
            columns[j] = columns[j] * inverse
            for later in range(j + 1, panel):
                weight = columns[j][first + later : first + later + 1, :]
                columns[later] = columns[later] - columns[j] * weight
                rows[later] = rows[later] - rows[j] * weight
        reduced = work
        for j in range(panel):
            reduced = reduced - columns[j] * rows[j]
        work = jnp.where(row_id >= first + panel, reduced, work)
        for j, k in enumerate(spots):
            work = jnp.where(row_id == k, rows[j], work)
    upper = jnp.where(row_id[:, :size] <= lane_id[:, :size], work[:, :size], 0.0)
    return upper, work[:, size:]


def finish_kernel(gram_ref, own_ref, image_ref, second_ref, next_ref, diag_ref, offdiag_ref):
    total = image_ref.shape[0] // 4
    vecs = diag_ref.shape[1]
    comps = next_ref.shape[0]
    zero = jnp.zeros((vecs, vecs), jnp.float32)
    eye = (
        lax.broadcasted_iota(jnp.int32, (vecs, vecs), 0)
        == lax.broadcasted_iota(jnp.int32, (vecs, vecs), 1)
    ).astype(jnp.float32)

    def grid(rows):
        return jnp.concatenate([jnp.concatenate(row, axis=1) for row in rows], axis=0)

    def block(matrix, row, column):
        return matrix[row * vecs : (row + 1) * vecs, column * vecs : (column + 1) * vecs]

    moments = unpack_moments(gram_ref[...], vecs)
    gram = grid([moments[k : k + 3] for k in range(3)])
    upper_0, inverse_0 = eliminate(block(gram, 0, 0))
    spread = grid([[inverse_0, zero, zero], [zero, inverse_0, zero], [zero, zero, inverse_0]])
    krylov = dot_both(dot_rows(spread, gram), spread)
    alpha_1, alpha_1_t = block(krylov, 0, 1), block(krylov, 1, 0)
    change = grid([[eye, zero, zero], [-alpha_1_t, eye, zero], [zero, -alpha_1_t, eye]])
    moved = dot_both(dot_rows(change, krylov), change)
    upper_1, inverse_1 = eliminate(block(moved, 1, 1))
    second = grid([[zero, inverse_1, zero], [-upper_1, zero, inverse_1]])
    products = dot_both(dot_rows(second, moved), second)
    alpha_2, alpha_2_t = block(products, 0, 1), block(products, 1, 0)
    upper_2, inverse_2 = eliminate(block(products, 1, 1) - dot_rows(alpha_2_t, alpha_2))
    residual = jnp.concatenate([-upper_1, -dot_rows(alpha_2_t, inverse_1), inverse_1], axis=1)
    coefs = dot_rows(dot_rows(dot_rows(inverse_2, residual), change), spread)
    diag_ref[0] = alpha_1
    diag_ref[1] = alpha_2
    offdiag_ref[0] = upper_0
    offdiag_ref[1] = upper_1
    offdiag_ref[2] = upper_2
    for comp in range(comps):
        for floor in range(2):
            parts = (
                (own_ref, floor * total),
                (image_ref, (1 + floor) * total),
                (second_ref, floor * total),
            )
            for across in range(0, SUB, 2):
                mixed = dot_rows(coefs, paired_rows(parts, comp * vecs, vecs, across))
                next_ref[comp, :, floor, across, :] = mixed[:, :LANE]
                next_ref[comp, :, floor, across + 1, :] = mixed[:, LANE:]


def finish(gram, blocks, out_shape, vecs):
    return call_whole(
        finish_kernel,
        [
            jax.ShapeDtypeStruct(out_shape, jnp.float32),
            jax.ShapeDtypeStruct((2, vecs, vecs), jnp.float32),
            jax.ShapeDtypeStruct((3, vecs, vecs), jnp.float32),
        ],
        gram, *blocks,
    )


def spread_sum(value, axes):
    copies = jnp.broadcast_to(value, (lax.axis_size(axes),) + value.shape)
    return jnp.sum(lax.all_to_all(copies, axes, 0, 0), axis=0)


def mesh_sum(value):
    value = value + lax.ppermute(value, "core", [(0, 1), (1, 0)])
    value = spread_sum(value, ("x", "dom"))
    return spread_sum(value, ("z",))


def shifted(value, axis, steps, wrap):
    size = lax.axis_size(axis)
    route = [(i, (i + steps) % size) for i in range(size) if wrap or 0 <= i + steps < size]
    return lax.ppermute(value, axis, route)


def gathered(elem_grad, elem_stress, elem_grade):
    capacity = elem_grad.shape[2]
    packed = jnp.concatenate(
        [
            elem_grad.reshape(24, capacity),
            elem_stress,
            elem_grade.astype(jnp.float32)[None],
            jnp.zeros((1, capacity), jnp.float32),
        ],
        axis=0,
    )
    ahead, behind = shifted(packed, "dom", 1, True), shifted(packed, "dom", -1, True)
    low, high = shifted(ahead[:16], "dom", 1, True), shifted(behind[16:], "dom", -1, True)
    return [packed, ahead, low, high, behind]


def per_device(
    elem_grad,
    elem_stress,
    elem_grade,
    grade_scale,
    part_counts,
    node_lists,
    stiff_diag,
    start_block,
):
    comps, vecs = start_block.shape[:2]
    total = comps * vecs
    own, edges = split_slab(start_block, stiff_diag)
    sources = gathered(elem_grad, elem_stress, elem_grade)
    from_left = shifted(edges[2:], "dom", 1, True)
    from_right = shifted(edges[:2], "dom", -1, True)
    columns = jnp.concatenate([from_left, from_right], axis=0)
    under = shifted(own, SLAB, 1, False)
    over = shifted(own, SLAB, -1, False)
    moment = start_gram(own, vecs)
    sources, under, over, moment = lax.optimization_barrier((sources, under, over, moment))
    low, top, below = local_stencils(part_counts, grade_scale, node_lists, sources)
    from_above = shifted(jnp.concatenate([low, below, columns], axis=0), SLAB, -1, False)
    from_below = shifted(jnp.concatenate([top, columns], axis=0), SLAB, 1, False)
    image, left, right, high = apply_first(
        under, own, over, low, top, below, from_above, from_below, columns, total
    )
    from_left = shifted(right, "dom", 1, True)
    from_right = shifted(left, "dom", -1, True)
    outer = first_gram(own, image, vecs)
    second, packed = apply_second(
        image, from_left, from_right, low, high, stiff_diag, moment, outer
    )
    dof_count = (
        start_block.size // vecs * lax.axis_size(SLAB + ("dom",))
    )
    packed = mesh_sum(packed) / dof_count
    return finish(packed, (own, image, second), start_block.shape, vecs)


def solution(mesh):
    torus = Mesh(mesh.devices.reshape(8, 4, 2, 4), SLAB + ("dom",))
    in_specs = (
        P(None, None, SLAB + ("dom",)),
        P(None, SLAB + ("dom",)),
        P(SLAB + ("dom",)),
        P(),
        P(SLAB, None),
        P(None, SLAB, None, "dom"),
        P(None, SLAB, None, "dom"),
        P(None, None, SLAB, None, "dom"),
    )
    out_specs = (P(None, None, SLAB, None, "dom"), P(), P())
    return jax.shard_map(
        per_device, mesh=torus, in_specs=in_specs, out_specs=out_specs, check_vma=False
    )
```

```python
import jax
import jax.numpy as jnp
from jax import lax
from jax.experimental import pallas as pl
from jax.experimental.pallas import tpu as pltpu
from jax.sharding import Mesh
from jax.sharding import PartitionSpec as P

highest = lax.Precision.HIGHEST
SUB, LANE = 8, 128
ROWS = 31
UNITS = 3
SLAB = ("z", "x", "core")


def lane_pick(values, index):
    return jnp.take_along_axis(values, index, axis=1, mode="promise_in_bounds")


def stencil_kernel(counts_ref, table_ref, lists_ref, *refs):
    sources, (low_ref, top_ref, below_ref, picked_ref) = refs[:-4], refs[-4:]
    sub = lax.broadcasted_iota(jnp.int32, (SUB, LANE), 0)
    lane = lax.broadcasted_iota(jnp.int32, (SUB, LANE), 1)
    inner = sub < SUB - 1
    ids = []
    for layer in range(2):
        behind = jnp.broadcast_to(lists_ref[2, layer, :, 0:1], (SUB, LANE))
        behind = jnp.max(jnp.where(lane == sub, behind, -1), axis=0, keepdims=True)
        behind = jnp.broadcast_to(behind, (SUB, LANE))
        behind = jnp.where(lane < SUB - 1, behind, -1)
        ids.append(jnp.where(inner, lists_ref[0, layer], behind))
    picked_ref[...] = jnp.zeros(picked_ref.shape, jnp.float32)
    parts = 4
    for part in range(parts):
        owner = lax.rem(lax.axis_index("dom") + (parts - part), parts)
        count = counts_ref[0, owner]
        start = jnp.int32(0)
        for other in range(parts):
            start = start + jnp.where(owner > other, counts_ref[0, other], 0)
        group_of, lane_of = [], []
        for layer in range(2):
            place = ids[layer] - start
            held = (place >= 0) & (place < count)
            group_of.append(jnp.where(held, place >> 7, -1))
            lane_of.append(jnp.where(held, place & (LANE - 1), 0))
        halves = ((0,), (1,), (2, 3), (4,))[part]

        def pick_groups(step, carry):
            spans, here = [], []
            for unit in range(UNITS):
                group = step * UNITS + unit
                spans.append(pl.ds(pl.multiple_of(group * LANE, LANE), LANE))
                here.append([group_of[layer] == group for layer in range(2)])
            for row in range(ROWS):
                half, line = divmod(row, 16) if len(halves) == 2 else (0, row)
                source = sources[halves[half]]
                found = [picked_ref[layer, row] for layer in range(2)]
                for unit in range(UNITS):
                    values = jnp.broadcast_to(source[line : line + 1, spans[unit]], (SUB, LANE))
                    for layer in range(2):
                        got = lane_pick(values, lane_of[layer])
                        found[layer] = jnp.where(here[unit][layer], got, found[layer])
                for layer in range(2):
                    picked_ref[layer, row] = found[layer]
            return carry

        width = UNITS * LANE
        lax.fori_loop(0, (count + width - 1) // width, pick_groups, 0)
    low_ref[...] = jnp.zeros(low_ref.shape, jnp.float32)
    top_ref[...] = jnp.zeros(top_ref.shape, jnp.float32)
    below_ref[...] = jnp.zeros(below_ref.shape, jnp.float32)
    first_lane = lane == 0

    def from_behind(rows):
        edge = lane_pick(jnp.broadcast_to(rows[SUB - 1 : SUB], (SUB, LANE)), sub)
        return jnp.where(first_lane, edge, pltpu.roll(rows, 1, axis=1))

    for layer in range(2):
        grade = picked_ref[layer, 30]
        scale = jnp.zeros((SUB, LANE), jnp.float32)
        for level in range(table_ref.shape[0]):
            scale = jnp.where(grade == float(level), table_ref[level], scale)
        own = [picked_ref[layer, row] for row in range(24)]
        own += [picked_ref[layer, 24 + row] * scale for row in range(6)]
        behind = [from_behind(rows) for rows in own]
        for slot in range(4):
            data = own if slot < 2 else behind
            stress = [jnp.where(inner, data[24 + row], 0.0) for row in range(6)]
            grad = data[:24]
            if slot % 2 == 1:
                stress = [pltpu.roll(rows, 1, axis=0) for rows in stress]
                grad = [pltpu.roll(rows, 1, axis=0) for rows in grad]
            order = ((0, 5, 4), (5, 1, 3), (4, 3, 2))
            for corner in range(8):
                pushed = [
                    stress[order[i][0]] * grad[corner]
                    + stress[order[i][1]] * grad[8 + corner]
                    + stress[order[i][2]] * grad[16 + corner]
                    for i in range(3)
                ]
                offset = (corner % 2 - slot % 2 + 1) + 3 * (corner // 2 % 2 - slot // 2 + 1)
                offset += 9 * (corner // 4)
                upper = sum(grad[8 * i + slot + 4] * pushed[i] for i in range(3))
                lower = sum(grad[8 * i + slot] * pushed[i] for i in range(3))
                if layer == 0:
                    low_ref[offset] += upper
                    below_ref[offset] += lower
                else:
                    top_ref[offset] += upper
                    low_ref[offset + 9] += lower
    for ref in (low_ref, top_ref, below_ref):
        for offset in range(ref.shape[0]):
            if offset % 3 != 1:
                ref[offset] = pltpu.roll(ref[offset], (offset % 3 - 1) % SUB, axis=0)


def local_stencils(counts, table, lists, sources):
    vmem = pl.BlockSpec(memory_space=pltpu.VMEM)
    smem = pl.BlockSpec(memory_space=pltpu.SMEM)
    return pl.pallas_call(
        stencil_kernel,
        out_shape=[
            jax.ShapeDtypeStruct((27, SUB, LANE), jnp.float32),
            jax.ShapeDtypeStruct((18, SUB, LANE), jnp.float32),
            jax.ShapeDtypeStruct((18, SUB, LANE), jnp.float32),
        ],
        in_specs=[smem, smem] + [vmem] * (1 + len(sources)),
        out_specs=[vmem, vmem, vmem],
        scratch_shapes=[pltpu.VMEM((2, ROWS, SUB, LANE), jnp.float32)],
        compiler_params=pltpu.CompilerParams(vmem_limit_bytes=24 * 1024 * 1024),
    )(counts, table, lists, *sources)


def split_kernel(start_ref, diag_ref, slab_ref, edges_ref):
    comps, vecs = start_ref.shape[:2]
    total = comps * vecs
    lane = lax.broadcasted_iota(jnp.int32, (SUB, LANE), 1)
    found = [jnp.zeros((SUB, LANE), jnp.float32)] * 4
    for comp in range(comps):
        for floor in range(2):
            slab_ref[2 * total + 2 * comp + floor] = diag_ref[comp, floor]

        def step(vec, carry):
            out = []
            place = comp * vecs + vec
            for floor in range(2):
                rows = start_ref[comp, vec, floor]
                slab_ref[floor * total + place] = rows
                out.append(jnp.where(lane == place, pltpu.roll(rows, place, axis=1), carry[floor]))
            for floor in range(2):
                rows = start_ref[comp, vec, floor]
                turned = pltpu.roll(rows, place + 1, axis=1)
                out.append(jnp.where(lane == place, turned, carry[2 + floor]))
            return tuple(out)

        found = lax.fori_loop(0, vecs, step, tuple(found), unroll=16)
    for k in range(4):
        edges_ref[k] = found[k]


def split_slab(start_block, diagonal):
    total = start_block.shape[0] * start_block.shape[1]
    return call_whole(
        split_kernel,
        [
            jax.ShapeDtypeStruct((2 * total + 2 * start_block.shape[0], SUB, LANE), jnp.float32),
            jax.ShapeDtypeStruct((4, SUB, LANE), jnp.float32),
        ],
        start_block, diagonal,
    )


def operator_rows(floors, behind, ahead, taps, weights, outs, edges, total, vecs, width):
    lane = lax.broadcasted_iota(jnp.int32, (SUB, LANE), 1)

    def step(index, carry):
        first = index * width
        rows = []
        for unit in range(width):
            vec = first + unit
            for z, (ref, base) in enumerate(floors):
                mid = ref[base + vec]
                left = pltpu.roll(behind[z], LANE - vec, axis=1)
                left = jnp.where(lane == 0, left, pltpu.roll(mid, 1, axis=1))
                right = pltpu.roll(ahead[z], LANE - 1 - vec, axis=1)
                right = jnp.where(lane == LANE - 1, right, pltpu.roll(mid, LANE - 1, axis=1))
                rows.append((left, mid, right))
        new = list(carry)
        comp = first // vecs
        for floor, (out_ref, base) in enumerate(outs):
            weight = weights[floor](comp)
            sums = [[None] * 3 for _ in range(width)]
            for offset in range(27):
                tap = taps[floor][offset]
                dx, dy, dz = offset % 3, offset // 3 % 3, offset // 9
                for unit in range(width):
                    term = tap * rows[len(floors) * unit + floor + dz][dy]
                    old = sums[unit][dx]
                    sums[unit][dx] = term if old is None else old + term
            for unit in range(width):
                vec = first + unit
                result = weight * rows[len(floors) * unit + floor + 1][1] + sums[unit][1]
                result = result + pltpu.roll(sums[unit][0], 1, axis=0)
                result = result + pltpu.roll(sums[unit][2], SUB - 1, axis=0)
                out_ref[base + vec] = result
                if edges is not None:
                    for side in range(2):
                        turned = pltpu.roll(result, vec + side, axis=1)
                        spot = 2 * floor + side
                        new[spot] = jnp.where(lane == vec, turned, new[spot])
        return tuple(new)

    zero = jnp.zeros((SUB, LANE), jnp.float32)
    count = 0 if edges is None else 2 * len(outs)
    done = lax.fori_loop(0, total // width, step, (zero,) * count)
    if edges is not None:
        for floor in range(len(outs)):
            edges[0][floor] = done[2 * floor]
            edges[1][floor] = done[2 * floor + 1]


def first_operator_kernel(
    under_ref, own_ref, over_ref, low_ref, top_ref, below_ref, from_above_ref, from_below_ref,
    columns_ref, image_ref, left_ref, right_ref, high_ref, under_taps_ref,
):
    total = image_ref.shape[0] // 4
    comps = (own_ref.shape[0] - 2 * total) // 2
    diag_row = 2 * total
    inside = jnp.where(sum(lax.axis_index(name) for name in SLAB) > 0, 1.0, 0.0)
    cols_refs = ((from_below_ref, 18), (columns_ref, 0), (from_above_ref, 45))
    high_ref[0:18] = top_ref[...]
    high_ref[18:27] = from_above_ref[36:45]
    high_ref[9:18] = high_ref[9:18] + from_above_ref[27:36]
    under_taps_ref[0:9] = from_below_ref[0:9] * inside
    under_taps_ref[9:18] = (from_below_ref[9:18] + below_ref[0:9]) * inside
    under_taps_ref[18:27] = below_ref[9:18] * inside
    slabs = (under_ref, own_ref, over_ref)
    floors = [(ref, floor * total) for ref in slabs for floor in range(2)]
    behind = [ref[row + floor] for ref, row in cols_refs for floor in range(2)]
    ahead = [ref[row + 2 + floor] for ref, row in cols_refs for floor in range(2)]

    def weight(ref, floor):
        return lambda comp: ref[diag_row + 2 * comp + floor]

    operator_rows(
        floors, behind, ahead, (under_taps_ref, low_ref, high_ref, from_above_ref),
        (weight(under_ref, 1), weight(own_ref, 0), weight(own_ref, 1), weight(over_ref, 0)),
        [(image_ref, floor * total) for floor in range(4)],
        (left_ref, right_ref), total, total // comps, 8,
    )


def second_operator_kernel(
    image_ref, from_left_ref, from_right_ref, low_ref, high_ref, diag_ref, moment_ref, outer_ref,
    out_ref, packed_ref,
):
    total = out_ref.shape[0] // 2
    comps = diag_ref.shape[0]
    vecs = total // comps

    def weight(floor):
        return lambda comp: diag_ref[comp, floor]

    operator_rows(
        [(image_ref, floor * total) for floor in range(4)],
        [from_left_ref[floor] for floor in range(4)],
        [from_right_ref[floor] for floor in range(4)],
        (low_ref, high_ref), (weight(0), weight(1)),
        [(out_ref, floor * total) for floor in range(2)],
        None, total, vecs, 16,
    )
    blocks = [
        ((image_ref, (1 + floor) * total), (out_ref, floor * total)) for floor in range(2)
    ]
    inner = local_gram(blocks, comps, vecs, vecs)
    outer = outer_ref[...]
    pack_moments(
        packed_ref, moment_ref[...], outer[:vecs], outer[vecs:], inner[:vecs], inner[vecs:]
    )


def square_ids(size):
    return (
        lax.broadcasted_iota(jnp.int32, (size, size), 0),
        lax.broadcasted_iota(jnp.int32, (size, size), 1),
    )


def pack_moments(packed_ref, *moments):
    size = moments[0].shape[0]
    half = size // 2
    row, column = square_ids(size)
    squares = [
        jnp.where(row <= column, moments[0], moments[1]),
        jnp.where(row <= column, moments[2], moments[3]),
    ]
    extra = jnp.zeros((size, size), jnp.float32)
    for k in range(2):
        line = jnp.sum(jnp.where(row == column, moments[2 * k + 1], 0.0), axis=0, keepdims=True)
        turned = jnp.concatenate([line[:, half:], line[:, :half]], axis=1)
        extra = jnp.where(row == half + 2 * k, line, extra)
        extra = jnp.where(row == half + 2 * k + 1, turned, extra)
    squares.append(jnp.where(row <= column, moments[4], extra))
    for k, square in enumerate(squares):
        packed_ref[SUB * k : SUB * (k + 1)] = jnp.concatenate(
            [square[SUB * part : SUB * (part + 1)] for part in range(size // SUB)], axis=1
        )


def unpack_moments(packed, size):
    half = size // 2
    row, column = square_ids(size)
    squares = [
        jnp.concatenate(
            [
                packed[SUB * k : SUB * (k + 1), size * part : size * (part + 1)]
                for part in range(size // SUB)
            ],
            axis=0,
        )
        for k in range(3)
    ]
    flipped = dot_both((row == column).astype(jnp.float32), jnp.concatenate(squares, axis=0))
    moments = []
    for k, square in enumerate(squares):
        mirror = flipped[:, size * k : size * (k + 1)]
        moments.append(jnp.where(row <= column, square, mirror))
        if k < 2:
            spot = half + 2 * k
            line = jnp.concatenate(
                [squares[2][spot : spot + 1, :half], squares[2][spot + 1 : spot + 2, :half]],
                axis=1,
            )
            lower = jnp.where(row > column, square, mirror)
            moments.append(jnp.where(row == column, line, lower))
    return moments


def paired_rows(parts, start, vecs, across):
    rows = []
    for ref, base in parts:
        span = pl.ds(base + start, vecs)
        rows.append(jnp.concatenate([ref[span, across, :], ref[span, across + 1, :]], axis=1))
    return jnp.concatenate(rows, axis=0)


def local_gram(blocks, comps, vecs, skipped):
    gram = None
    for comp in range(comps):
        for parts in blocks:
            for across in range(0, SUB, 2):
                rows = paired_rows(parts, comp * vecs, vecs, across)
                term = dot_both(rows, rows[skipped:])
                gram = term if gram is None else gram + term
    return gram


def start_gram_kernel(own_ref, gram_ref):
    vecs = gram_ref.shape[0]
    total = own_ref.shape[0] * vecs // (2 * vecs + 2)
    blocks = [((own_ref, floor * total),) for floor in range(2)]
    gram_ref[...] = local_gram(blocks, total // vecs, vecs, 0)


def first_gram_kernel(own_ref, image_ref, gram_ref):
    vecs = gram_ref.shape[1]
    total = image_ref.shape[0] // 4
    blocks = [
        ((own_ref, floor * total), (image_ref, (1 + floor) * total)) for floor in range(2)
    ]
    gram_ref[...] = local_gram(blocks, total // vecs, vecs, vecs)


def call_whole(kernel, out_shape, *operands, scratch_shapes=()):
    vmem = pl.BlockSpec(memory_space=pltpu.VMEM)
    return pl.pallas_call(
        kernel,
        out_shape=out_shape,
        in_specs=[vmem] * len(operands),
        out_specs=[vmem] * len(out_shape),
        scratch_shapes=scratch_shapes,
        compiler_params=pltpu.CompilerParams(vmem_limit_bytes=32 * 1024 * 1024),
    )(*operands)


def apply_first(under, own, over, low, top, below, from_above, from_below, columns, total):
    edge = jax.ShapeDtypeStruct((4, SUB, LANE), jnp.float32)
    taps = jax.ShapeDtypeStruct((27, SUB, LANE), jnp.float32)
    return call_whole(
        first_operator_kernel,
        [jax.ShapeDtypeStruct((4 * total, SUB, LANE), jnp.float32), edge, edge, taps],
        under, own, over, low, top, below, from_above, from_below, columns,
        scratch_shapes=[pltpu.VMEM((27, SUB, LANE), jnp.float32)],
    )


def apply_second(image, from_left, from_right, low, high, diagonal, moment, outer):
    total = image.shape[0] // 4
    vecs = total // diagonal.shape[0]
    return call_whole(
        second_operator_kernel,
        [
            jax.ShapeDtypeStruct((2 * total, SUB, LANE), jnp.float32),
            jax.ShapeDtypeStruct((3 * SUB, SUB * vecs // 2), jnp.float32),
        ],
        image, from_left, from_right, low, high, diagonal, moment, outer,
    )


def start_gram(own, vecs):
    return call_whole(start_gram_kernel, [jax.ShapeDtypeStruct((vecs, vecs), jnp.float32)], own)[0]


def first_gram(own, image, vecs):
    shape = jax.ShapeDtypeStruct((2 * vecs, vecs), jnp.float32)
    return call_whole(first_gram_kernel, [shape], own, image)[0]


def dot_rows(left, right):
    return lax.dot_general(
        left, right, (((1,), (0,)), ((), ())), precision=highest, preferred_element_type=jnp.float32
    )


def dot_both(left, right):
    return lax.dot_general(
        left, right, (((1,), (1,)), ((), ())), precision=highest, preferred_element_type=jnp.float32
    )


def eliminate(gram):
    size = gram.shape[0]
    row_id = lax.broadcasted_iota(jnp.int32, (size, 2 * size), 0)
    lane_id = lax.broadcasted_iota(jnp.int32, (size, 2 * size), 1)
    identity = (row_id[:, :size] == lane_id[:, :size]).astype(jnp.float32)
    work = jnp.concatenate([gram, identity], axis=1)
    panel = 16
    for first in range(0, size, panel):
        spots = range(first, first + panel)
        columns = [jnp.broadcast_to(work[:, k : k + 1], (size, 2 * size)) for k in spots]
        rows = [work[k : k + 1, :] for k in spots]
        for j, k in enumerate(spots):
            pivot = columns[j][k : k + 1, :]
            inverse = lax.rsqrt(pivot)
            inverse = inverse * (1.5 - 0.5 * pivot * inverse * inverse)
            rows[j] = rows[j] * inverse
            columns[j] = columns[j] * inverse
            for later in range(j + 1, panel):
                weight = columns[j][first + later : first + later + 1, :]
                columns[later] = columns[later] - columns[j] * weight
                rows[later] = rows[later] - rows[j] * weight
        reduced = work
        for j in range(panel):
            reduced = reduced - columns[j] * rows[j]
        work = jnp.where(row_id >= first + panel, reduced, work)
        for j, k in enumerate(spots):
            work = jnp.where(row_id == k, rows[j], work)
    upper = jnp.where(row_id[:, :size] <= lane_id[:, :size], work[:, :size], 0.0)
    return upper, work[:, size:]


def finish_kernel(gram_ref, own_ref, image_ref, second_ref, next_ref, diag_ref, offdiag_ref):
    total = image_ref.shape[0] // 4
    vecs = diag_ref.shape[1]
    comps = next_ref.shape[0]
    zero = jnp.zeros((vecs, vecs), jnp.float32)
    eye = (
        lax.broadcasted_iota(jnp.int32, (vecs, vecs), 0)
        == lax.broadcasted_iota(jnp.int32, (vecs, vecs), 1)
    ).astype(jnp.float32)

    def grid(rows):
        return jnp.concatenate([jnp.concatenate(row, axis=1) for row in rows], axis=0)

    def block(matrix, row, column):
        return matrix[row * vecs : (row + 1) * vecs, column * vecs : (column + 1) * vecs]

    moments = unpack_moments(gram_ref[...], vecs)
    gram = grid([moments[k : k + 3] for k in range(3)])
    upper_0, inverse_0 = eliminate(block(gram, 0, 0))
    spread = grid([[inverse_0, zero, zero], [zero, inverse_0, zero], [zero, zero, inverse_0]])
    krylov = dot_both(dot_rows(spread, gram), spread)
    alpha_1, alpha_1_t = block(krylov, 0, 1), block(krylov, 1, 0)
    change = grid([[eye, zero, zero], [-alpha_1_t, eye, zero], [zero, -alpha_1_t, eye]])
    moved = dot_both(dot_rows(change, krylov), change)
    upper_1, inverse_1 = eliminate(block(moved, 1, 1))
    second = grid([[zero, inverse_1, zero], [-upper_1, zero, inverse_1]])
    products = dot_both(dot_rows(second, moved), second)
    alpha_2, alpha_2_t = block(products, 0, 1), block(products, 1, 0)
    upper_2, inverse_2 = eliminate(block(products, 1, 1) - dot_rows(alpha_2_t, alpha_2))
    residual = jnp.concatenate([-upper_1, -dot_rows(alpha_2_t, inverse_1), inverse_1], axis=1)
    coefs = dot_rows(inverse_2, dot_rows(residual, dot_rows(change, spread)))
    diag_ref[0] = alpha_1
    diag_ref[1] = alpha_2
    offdiag_ref[0] = upper_0
    offdiag_ref[1] = upper_1
    offdiag_ref[2] = upper_2
    for comp in range(comps):
        for floor in range(2):
            parts = (
                (own_ref, floor * total),
                (image_ref, (1 + floor) * total),
                (second_ref, floor * total),
            )
            for across in range(0, SUB, 2):
                mixed = dot_rows(coefs, paired_rows(parts, comp * vecs, vecs, across))
                next_ref[comp, :, floor, across, :] = mixed[:, :LANE]
                next_ref[comp, :, floor, across + 1, :] = mixed[:, LANE:]


def finish(gram, blocks, out_shape, vecs):
    return call_whole(
        finish_kernel,
        [
            jax.ShapeDtypeStruct(out_shape, jnp.float32),
            jax.ShapeDtypeStruct((2, vecs, vecs), jnp.float32),
            jax.ShapeDtypeStruct((3, vecs, vecs), jnp.float32),
        ],
        gram, *blocks,
    )


def spread_sum(value, axes):
    copies = jnp.broadcast_to(value, (lax.axis_size(axes),) + value.shape)
    return jnp.sum(lax.all_to_all(copies, axes, 0, 0), axis=0)


def mesh_sum(value):
    value = value + lax.ppermute(value, "core", [(0, 1), (1, 0)])
    value = spread_sum(value, ("x", "dom"))
    return spread_sum(value, ("z",))


def shifted(value, axis, steps, wrap):
    size = lax.axis_size(axis)
    route = [(i, (i + steps) % size) for i in range(size) if wrap or 0 <= i + steps < size]
    return lax.ppermute(value, axis, route)


def gathered(elem_grad, elem_stress, elem_grade):
    capacity = elem_grad.shape[2]
    packed = jnp.concatenate(
        [
            elem_grad.reshape(24, capacity),
            elem_stress,
            elem_grade.astype(jnp.float32)[None],
            jnp.zeros((1, capacity), jnp.float32),
        ],
        axis=0,
    )
    ahead, behind = shifted(packed, "dom", 1, True), shifted(packed, "dom", -1, True)
    low, high = shifted(ahead[:16], "dom", 1, True), shifted(behind[16:], "dom", -1, True)
    return [packed, ahead, low, high, behind]


def per_device(
    elem_grad,
    elem_stress,
    elem_grade,
    grade_scale,
    part_counts,
    node_lists,
    stiff_diag,
    start_block,
):
    comps, vecs = start_block.shape[:2]
    total = comps * vecs
    own, edges = split_slab(start_block, stiff_diag)
    sources = gathered(elem_grad, elem_stress, elem_grade)
    from_left = shifted(edges[2:], "dom", 1, True)
    from_right = shifted(edges[:2], "dom", -1, True)
    columns = jnp.concatenate([from_left, from_right], axis=0)
    under = shifted(own, SLAB, 1, False)
    over = shifted(own, SLAB, -1, False)
    moment = start_gram(own, vecs)
    sources, under, over, moment = lax.optimization_barrier((sources, under, over, moment))
    low, top, below = local_stencils(part_counts, grade_scale, node_lists, sources)
    from_above = shifted(jnp.concatenate([low, below, columns], axis=0), SLAB, -1, False)
    from_below = shifted(jnp.concatenate([top, columns], axis=0), SLAB, 1, False)
    image, left, right, high = apply_first(
        under, own, over, low, top, below, from_above, from_below, columns, total
    )
    from_left = shifted(right, "dom", 1, True)
    from_right = shifted(left, "dom", -1, True)
    outer = first_gram(own, image, vecs)
    second, packed = apply_second(
        image, from_left, from_right, low, high, stiff_diag, moment, outer
    )
    dof_count = (
        start_block.size // vecs * lax.axis_size(SLAB + ("dom",))
    )
    packed = mesh_sum(packed) / dof_count
    return finish(packed, (own, image, second), start_block.shape, vecs)


def solution(mesh):
    torus = Mesh(mesh.devices.reshape(8, 4, 2, 4), SLAB + ("dom",))
    in_specs = (
        P(None, None, SLAB + ("dom",)),
        P(None, SLAB + ("dom",)),
        P(SLAB + ("dom",)),
        P(),
        P(SLAB, None),
        P(None, SLAB, None, "dom"),
        P(None, SLAB, None, "dom"),
        P(None, None, SLAB, None, "dom"),
    )
    out_specs = (P(None, None, SLAB, None, "dom"), P(), P())
    return jax.shard_map(
        per_device, mesh=torus, in_specs=in_specs, out_specs=out_specs, check_vma=False
    )
```
